32 devices in a mesh: group: 8 (over z, core), dp: 4 (over y, x).
Axes of the slice: x: 2, y: 2, z: 4, core: 2. Of those that a mesh axis runs over, the one named last changes fastest.
Arguments:
- resp_q: bfloat16 [8, 1024, 4096], P('group', 'dp'), may hold values from -410 to 410
- resp_k: bfloat16 [8, 1024, 4096], P('group', 'dp'), may hold values from -410 to 410
- resp_v: bfloat16 [8, 1024, 4096], P('group', 'dp'), may hold values from -6 to 6
- prompt_k: bfloat16 [8, 512, 4096], P('group', 'dp'), may hold values from -410 to 410
- prompt_v: bfloat16 [8, 512, 4096], P('group', 'dp'), may hold values from -6 to 6
- prompt_len: int32 [8], P('group'), may hold values from 128 to 512
- resp_len: int32 [8, 4], P('group', 'dp'), may hold values from 1 to 256, as said below
- assign: int32 [8, 8], P('group', 'dp'), may hold values from 0 to 15, as said below
- rewards: float32 [8, 4], P('group', 'dp'), may hold values from -18 to 18
- feat_q: bfloat16 [32, 128, 128], replicated, may hold values from -1 to 1
- feat_k: bfloat16 [32, 128, 128], replicated, may hold values from -1 to 1
Outputs:
- attn_out: bfloat16 [8, 512, 4096], P('group', 'dp')
- token_adv: float32 [8, 512], P('group', 'dp')
The draws below stay inside these ranges and needn't reach their ends.
Inputs may be any that keep to these rules, and one draw needn't show every extreme that they name: Response r of a prompt has ceil(resp_len / 64) live blocks; these counts sum to 2 * 4 over a prompt's responses, and one response of every prompt has 4 blocks. `assign`: entry d * 2 + j names the block r * 4 + c (block c of response r) whose outputs go to slot j of device d of dp. Every live block of the prompt is named exactly once, and the 2 slots of one device name blocks of different responses.
All inputs are finite; a program needn't handle non-finite values.
Results may differ from the reference program's by a relative error of at most 0.0085.
Values may be sent and summed in bfloat16 or wider, within the bound.
A program may use at most 128 MiB of HBM per device.

```python
import jax
import jax.numpy as jnp
from jax import lax

H = 32
DH = 128
FH = 128
BLK = 64
MAXC = 4
CAP = 2
PT_DEV = 128
PROMPTS = 8
RESP = 4


def heavy_draw(key, rows, salt):
    stream = jax.random.fold_in(key, salt)
    first_key = jax.random.fold_in(stream, 0)
    extent = (PROMPTS, rows, H * DH)
    sample = jnp.clip(jax.random.normal(first_key, extent, jnp.float32), -6.0, 6.0)
    return sample.astype(jnp.bfloat16)


def draw_resp_q(key, part):
    return heavy_draw(key, RESP * MAXC * BLK, 101)


def draw_resp_k(key, part):
    return heavy_draw(key, RESP * MAXC * BLK, 202)


def draw_prompt_k(key, part):
    return heavy_draw(key, RESP * PT_DEV, 303)


def draw_rewards(key, part):
    stream = jax.random.fold_in(key, 404)
    first_key = jax.random.fold_in(stream, 0)
    rising = 1.0 + 2.0 * jnp.arange(PROMPTS, dtype=jnp.float32)[:, None] / (PROMPTS - 1)
    sample = jnp.clip(jax.random.normal(first_key, (PROMPTS, RESP), jnp.float32), -6.0, 6.0) * rising
    return sample


def stretch_plan(key):

    def per_prompt(prompt_key):
        slot_key, lead_key, tail_key, order_key, device_key = jax.random.split(prompt_key, 5)
        slots = RESP * (MAXC - 1)
        counter = jnp.arange(slots, dtype=jnp.int32)
        ranking = jax.random.randint(slot_key, (slots,), 0, 1 << 20).astype(jnp.int32) * slots + counter
        leader = jax.random.randint(lead_key, (), 0, RESP).astype(jnp.int32)
        owner = counter // (MAXC - 1)
        ranking = jnp.where(owner == leader, (1 << 20) * slots + counter, ranking)
        ordering = jnp.argsort(-ranking)
        chosen = jnp.zeros((slots,), jnp.int32).at[ordering[:RESP * (CAP - 1)]].set(1)
        blocks = 1 + chosen.reshape(RESP, MAXC - 1).sum(axis=1)
        tails = jax.random.randint(tail_key, (RESP,), 1, BLK + 1).astype(jnp.int32)
        tokens = (blocks - 1) * BLK + tails
        index_row = jnp.arange(RESP, dtype=jnp.int32)
        sigma = jnp.argsort(jax.random.randint(order_key, (RESP,), 0, 1 << 20).astype(jnp.int32) * RESP + index_row)
        devperm = jnp.argsort(jax.random.randint(device_key, (RESP,), 0, 1 << 20).astype(jnp.int32) * RESP + index_row)
        ordered = blocks[sigma]
        starts = jnp.cumsum(ordered) - ordered
        stream_index = jnp.arange(RESP * CAP, dtype=jnp.int32)
        located = jnp.sum((starts[None, :] <= stream_index[:, None]).astype(jnp.int32), axis=1) - 1
        response = sigma[located]
        within = stream_index - starts[located]
        target = devperm[stream_index % RESP] * CAP + stream_index // RESP
        table = jnp.zeros((RESP * CAP,), jnp.int32).at[target].set((response * MAXC + within).astype(jnp.int32))
        return (tokens.astype(jnp.int32), table)
    prompt_keys = jax.random.split(jax.random.fold_in(key, 505), PROMPTS)
    return jax.vmap(per_prompt)(prompt_keys)


def draw_resp_len(key, part):
    return stretch_plan(key)[0]


def draw_assign(key, part):
    return stretch_plan(key)[1]


def set_ends(result, stream_key, least, top_value):
    longest = result.shape.index(max(result.shape))
    spots = []
    for shift in (0, 1):
        where = [jax.random.randint(jax.random.fold_in(stream_key, axis), (), 0, length) for axis, length in enumerate(result.shape)]
        where[longest] = (where[longest] + shift) % result.shape[longest]
        spots.append(tuple(where))
    return result.at[spots[0]].set(least).at[spots[1]].set(top_value)


def steps_of(own_key, shape, shards, least, largest):
    def one(position, parts):
        heights = jax.random.uniform(jax.random.fold_in(jax.random.fold_in(own_key, 6), position), (parts,), jnp.float32, least / len(shards), largest / len(shards))
        return jnp.repeat(jnp.exp(heights), shape[position] // parts).reshape((-1,) + (1,) * (len(shape) - position - 1))

    level = one(*shards[0])
    for cut in shards[1:]:
        level = level * one(*cut)
    return level


def bell_draw(stream_key, dims, scale, reach, cuts=(), held_as=jnp.bfloat16):
    array = scale * jax.random.normal(stream_key, dims, jnp.float32)
    if cuts:
        array = array * steps_of(stream_key, dims, cuts, -0.22, 0.18)
    return jnp.clip(array, -reach, reach).astype(held_as)


def setup_inputs(seed: int = 0) -> dict:
    splits = jax.random.split(jax.random.key(seed), 12)
    resp_q = draw_resp_q(jax.random.fold_in(splits[11], 71), 0)
    resp_k = draw_resp_k(jax.random.fold_in(splits[11], 71), 0)
    resp_v = bell_draw(splits[2], (PROMPTS, RESP * MAXC * BLK, H * DH), 1.0, 6.0, ((0, 8), (1, 4)))
    prompt_k = draw_prompt_k(jax.random.fold_in(splits[11], 71), 0)
    prompt_v = bell_draw(splits[4], (PROMPTS, RESP * PT_DEV, H * DH), 1.0, 6.0, ((0, 8), (1, 4)))
    prompt_len = set_ends(jax.random.randint(splits[5], (PROMPTS,), RESP * PT_DEV // 4, RESP * PT_DEV + 1), jax.random.fold_in(splits[5], 1), RESP * PT_DEV // 4, RESP * PT_DEV).astype(jnp.int32)
    resp_len = draw_resp_len(jax.random.fold_in(splits[11], 71), 0)
    assign = draw_assign(jax.random.fold_in(splits[11], 71), 0)
    rewards = draw_rewards(jax.random.fold_in(splits[11], 71), 0)
    feat_q = bell_draw(splits[9], (H, DH, FH), (DH // 4) ** -0.5, 1.0)
    feat_k = bell_draw(splits[10], (H, DH, FH), (DH // 4) ** -0.5, 1.0)
    return dict(resp_q=resp_q, resp_k=resp_k, resp_v=resp_v, prompt_k=prompt_k, prompt_v=prompt_v, prompt_len=prompt_len, resp_len=resp_len, assign=assign, rewards=rewards, feat_q=feat_q, feat_k=feat_k)


def features(rows, weights):
    logits = jnp.einsum('thd,hdf->thf', rows.astype(jnp.float32), weights.astype(jnp.float32), precision=lax.Precision.HIGHEST)
    return jnp.concatenate([jax.nn.softmax(logits, axis=-1), jax.nn.softmax(-logits, axis=-1)], axis=-1).astype(jnp.bfloat16)

def reference(resp_q, resp_k, resp_v, prompt_k, prompt_v, prompt_len, resp_len, assign, rewards, feat_q, feat_k):
    head_count = feat_q.shape[0]
    head_width = feat_q.shape[1]
    length = MAXC * BLK
    prompt_rows = prompt_k.shape[1]
    causal = jnp.arange(length)[:, None] >= jnp.arange(length)[None, :]
    highest = lax.Precision.HIGHEST

    def per_prompt(operands):
        queries, key_rows, value_rows, prompt_keys, prompt_values, limit, lengths, slot_ids = operands
        prompt_feat = features(prompt_keys.reshape(prompt_rows, head_count, head_width), feat_k)
        keep = jnp.arange(prompt_rows) < limit
        masked = jnp.where(keep[:, None, None], prompt_feat.astype(jnp.float32), jnp.float32(0.0))
        kv_state = jnp.einsum('shf,she->hfe', masked, prompt_values.reshape(prompt_rows, head_count, head_width).astype(jnp.float32), precision=highest).astype(jnp.bfloat16)
        key_total = lax.optimization_barrier(jnp.sum(masked, axis=0)).astype(jnp.bfloat16)

        def per_response(items):
            query_rows, key_block, value_block, size = items
            query_feat = features(query_rows.reshape(length, head_count, head_width), feat_q).astype(jnp.float32)
            key_feat = features(key_block.reshape(length, head_count, head_width), feat_k).astype(jnp.float32)
            prompt_num = jnp.einsum('thf,hfe->the', query_feat, kv_state.astype(jnp.float32), precision=highest).astype(jnp.bfloat16)
            prompt_den = jnp.einsum('thf,hf->th', query_feat, key_total.astype(jnp.float32), precision=highest).astype(jnp.bfloat16)
            scores = jnp.einsum('thf,shf->hts', query_feat, key_feat, precision=highest)
            scores = jnp.where(causal[None], scores, jnp.float32(0.0))
            intra_den = lax.optimization_barrier(jnp.sum(scores, axis=-1))
            rounded = lax.optimization_barrier(scores.astype(jnp.bfloat16)).astype(jnp.float32)
            values_f = value_block.reshape(length, head_count, head_width).astype(jnp.float32)
            intra_num = jnp.einsum('hts,she->the', rounded, values_f, precision=highest)
            combined = (prompt_num.astype(jnp.float32) + intra_num) / (prompt_den.astype(jnp.float32) + intra_den.T)[:, :, None]
            live_rows = jnp.arange(length) < size
            combined = jnp.where(live_rows[:, None, None], combined, jnp.float32(0.0))
            return combined.astype(jnp.bfloat16).reshape(MAXC, BLK, head_count * head_width)
        outputs = lax.map(per_response, (queries.reshape(RESP, length, head_count * head_width), key_rows.reshape(RESP, length, head_count * head_width), value_rows.reshape(RESP, length, head_count * head_width), lengths))
        flat = outputs.reshape(RESP * MAXC, BLK, head_count * head_width)
        return jnp.take(flat, slot_ids.astype(jnp.int32), axis=0).reshape(RESP * CAP * BLK, head_count * head_width)
    attended = lax.map(per_prompt, (resp_q, resp_k, resp_v, prompt_k, prompt_v, prompt_len, resp_len, assign))
    centred = rewards - lax.optimization_barrier(jnp.mean(rewards, axis=1, keepdims=True))
    spread = jnp.mean(centred * centred)
    advantage = centred / jnp.sqrt(spread + 1e-06)
    responses = (assign // MAXC).astype(jnp.int32)
    pieces = (assign % MAXC).astype(jnp.int32)
    slot_adv = jnp.take_along_axis(advantage, responses, axis=1)
    slot_len = jnp.take_along_axis(resp_len, responses, axis=1)
    positions = pieces[:, :, None] * BLK + jnp.arange(BLK, dtype=jnp.int32)[None, None, :]
    token_adv = jnp.where(positions < slot_len[:, :, None], slot_adv[:, :, None], jnp.float32(0.0))
    return (attended, token_adv.reshape(rewards.shape[0], RESP * CAP * BLK))
```

```python
import functools

import jax
import jax.numpy as jnp
from jax import lax
from jax.experimental import pallas as pl
from jax.experimental.pallas import tpu as pltpu
from jax.sharding import PartitionSpec as P

BLK = 64
MESH = pl.DeviceIdType.MESH
NT = (((1,), (1,)), ((), ()))
NN = (((1,), (0,)), ((), ()))
F32 = jnp.float32
BF16 = jnp.bfloat16


def dot(a, b, dims=NN):
    return lax.dot_general(a, b, dims, preferred_element_type=F32)


def features(rows, weights, ones_blocks):
    logits = dot(rows, weights)
    top = jnp.max(logits, axis=-1, keepdims=True)
    low = jnp.min(logits, axis=-1, keepdims=True)
    both = jnp.concatenate([jnp.exp(logits - top), jnp.exp(low - logits)], axis=1)
    sums = dot(both.astype(BF16), ones_blocks)
    return (both * (1.0 / sums)).astype(BF16)


def kernel(
    n, across, groups, heads, chunks,
    plen, rlen, slots_sm, rew_sm, q_hbm, k_hbm, v_hbm, pk_hbm, pv_hbm, fq_hbm, fk_hbm,
    orecv, adv_ref,
    qs, ks, vs, fqs, fks, pks, pvs, part, first_in, passing, second_in, state,
    ptot32, ptot, phq, inum, ostage,
    tinfo, trew, tsm, gsum,
    load_sem, oself_sem, a_send, a_recv, b_send, b_recv, t_send, t_recv,
    st_send, st_recv, o_send, o_recv,
    i_send, i_recv, g_send, g_recv, sm_sem,
):
    me = lax.axis_index("dp")
    grp = lax.axis_index("group")
    rows = qs.shape[0]
    width = fqs.shape[1]
    feat = fqs.shape[2]
    pieces = rows // BLK
    slot_count = slots_sm.shape[1]
    own = heads // n
    per = own // chunks
    prows = pks.shape[0]

    down = n // across
    row = me // across
    col = me % across

    def peer(i):
        return (row + i // across) % down * across + (col + i % across) % across

    def source(i):
        return (row + down - i // across) % down * across + (col + across - i % across) % across

    loads = [
        pltpu.make_async_copy(src, dst, load_sem.at[i])
        for i, (src, dst) in enumerate(
            [
                (fk_hbm, fks), (pk_hbm.at[0], pks), (pv_hbm.at[0], pvs),
                (fq_hbm, fqs), (q_hbm.at[0], qs), (k_hbm.at[0], ks), (v_hbm.at[0], vs),
            ]
        )
    ]
    for copy in loads:
        copy.start()

    barrier = pltpu.get_barrier_semaphore()
    for i in range(1, n):
        pl.semaphore_signal(barrier, inc=1, device_id={"dp": peer(i)}, device_id_type=MESH)
    for i in range(1, groups):
        pl.semaphore_signal(
            barrier, inc=1, device_id={"group": lax.rem(grp + i, groups)}, device_id_type=MESH
        )

    lane = lax.broadcasted_iota(jnp.int32, (8, 128), 1)
    info = jnp.where(lane == slot_count, rlen[0, 0], 0)
    for j in range(slot_count):
        info = jnp.where(lane == j, slots_sm[0, j], info)
    tinfo[me] = info
    trew[me] = jnp.full((8, 128), rew_sm[0, 0], F32)

    def remote(src, dst, send, recv, axis, target):
        return pltpu.make_async_remote_copy(
            src_ref=src, dst_ref=dst, send_sem=send, recv_sem=recv,
            device_id={axis: target}, device_id_type=MESH,
        )

    def info_copies(i):
        return [
            remote(tinfo.at[me], tinfo.at[me], i_send.at[0, i], i_recv.at[0, i], "dp", peer(i)),
            remote(trew.at[me], trew.at[me], i_send.at[1, i], i_recv.at[1, i], "dp", peer(i)),
        ]

    def group_copy(i):
        return remote(
            gsum.at[grp], gsum.at[grp], g_send.at[i], g_recv.at[i], "group",
            lax.rem(grp + i, groups),
        )

    def total_copy(i):
        return remote(ptot.at[me], ptot.at[me], t_send.at[i], t_recv.at[i], "dp", peer(i))

    def sizes(c):
        return (across, down) if c % 2 == 0 else (down, across)

    def offset(c, one, two):
        return two * across + one if c % 2 == 0 else one * across + two

    def first_copy(c, i):
        span = pl.ds(0, sizes(c)[1])
        return remote(
            part.at[c, i, span], first_in.at[c, i - 1, span], a_send.at[c, i], a_recv.at[c, i],
            "dp", peer(offset(c, i, 0)),
        )

    def second_copy(c, i):
        return remote(
            passing.at[c, i - 1], second_in.at[c, i - 1], b_send.at[c, i], b_recv.at[c, i],
            "dp", peer(offset(c, 0, i)),
        )

    def state_copy(c, i):
        dr, dc = i // across, i % across
        if c % 2 == 0:
            target, holder = (dr * across, dc) if dr else (dc, 0)
        else:
            target, holder = (dc, dr * across) if dc else (dr * across, 0)
        chunk = state.at[source(holder), c]
        return remote(chunk, chunk, st_send.at[c, i], st_recv.at[c, i], "dp", peer(target))

    straight = [i for i in range(1, n) if i < across or i % across == 0]
    relayed = [i for i in range(1, n) if i not in straight]

    def feeds(c):
        return [i for i in straight if (i < across if c % 2 == 0 else i % across == 0)]

    def relay(c):
        for i in feeds(c):
            state_copy(c, i).wait_recv()
        for i in relayed:
            state_copy(c, i).start()

    def out_copy(c, g, i):
        cols = pl.ds((g * own + c * per) * width, per * width)
        src, dst = ostage.at[i, :, cols], orecv.at[me, :, cols]
        if i == 0:
            return pltpu.make_async_copy(src, dst, oself_sem.at[c, g])
        return remote(src, dst, o_send.at[c, g, i], o_recv.at[c, g, i], "dp", peer(i))

    left = lax.broadcasted_iota(jnp.int32, (2 * feat, 2 * feat), 0) < feat
    upper = lax.broadcasted_iota(jnp.int32, (2 * feat, 2 * feat), 1) < feat
    ones_blocks = jnp.where(left == upper, 1.0, 0.0).astype(BF16)

    keep = (
        lax.broadcasted_iota(jnp.int32, (width + 16, prows), 1) + me * prows < plen[0]
    )

    def partial_states(c):
        one_size, two_size = sizes(c)
        for one in [*range(1, one_size), 0]:
            for two in range(two_size):
                owner = peer(offset(c, one, two))

                def step(j, carry, c=c, one=one, two=two, owner=owner):
                    h = owner * own + c * per + j
                    cols = pl.ds(pl.multiple_of(h * width, 128), width)
                    kf = features(pks[:, cols], fks[h], ones_blocks)
                    values = jnp.concatenate(
                        [pvs[:, cols].T, jnp.ones((16, prows), BF16)], axis=0
                    )
                    values = jnp.where(keep, values.astype(F32), 0.0).astype(BF16)
                    found = dot(values, kf)
                    part[c, one, two, pl.ds(pl.multiple_of(j * width, 128), width), :] = found[
                        :width
                    ].astype(BF16)
                    ptot32[pl.ds(h, 1), :] = found[width : width + 1]
                    return carry

                lax.fori_loop(0, per, step, 0, unroll=True)

    def start_first(c):
        for i in range(1, sizes(c)[0]):
            first_copy(c, i).start()

    def lines(j):
        return pl.ds(pl.multiple_of(j * width, 128), width)

    def pass_on(c):
        one_size, two_size = sizes(c)
        for i in range(1, one_size):
            first_copy(c, i).wait_recv()
        for two in range(1, two_size):

            def step(j, carry, two=two):
                total = part[c, 0, two, lines(j), :].astype(F32)
                for i in range(1, one_size):
                    total = total + first_in[c, i - 1, two, lines(j), :].astype(F32)
                passing[c, two - 1, lines(j), :] = total.astype(BF16)
                return carry

            lax.fori_loop(0, per, step, 0)
            second_copy(c, two).start()

    def settle(c):
        one_size, two_size = sizes(c)
        for i in range(1, two_size):
            second_copy(c, i).wait_recv()

        def step(j, carry):
            total = part[c, 0, 0, lines(j), :].astype(F32)
            for i in range(1, one_size):
                total = total + first_in[c, i - 1, 0, lines(j), :].astype(F32)
            for i in range(1, two_size):
                total = total + second_in[c, i - 1, lines(j), :].astype(F32)
            state[me, c, lines(j), :] = total.astype(BF16)
            return carry

        lax.fori_loop(0, per, step, 0)
        for i in straight:
            state_copy(c, i).start()

    causal = lax.broadcasted_iota(jnp.int32, (rows, rows), 0) >= lax.broadcasted_iota(
        jnp.int32, (rows, rows), 1
    )

    def head_of(t):
        c = t // (n * per)
        return (t // per) % n * own + c * per + t % per

    def intra_head(h):
        cols = pl.ds(pl.multiple_of(h * width, 128), width)
        qf = features(qs[:, cols], fqs[h], ones_blocks)
        kf = features(ks[:, cols], fks[h], ones_blocks)
        phq[h] = qf
        scores = dot(qf, kf, NT)
        weight = jnp.where(causal, scores, 0.0).astype(BF16)
        value = jnp.concatenate([vs[:, cols], jnp.ones((rows, width), BF16)], axis=1)
        inum[h] = dot(weight, value)

    def intra(begin, end):
        def step(t, carry):
            intra_head(head_of(begin + 2 * t))
            intra_head(head_of(begin + 2 * t + 1))
            return carry

        lax.fori_loop(0, (end - begin) // 2, step, 0)

    def rewards_and_tables():
        for i in range(1, n):
            for copy in info_copies(i):
                copy.wait_recv()
        total_reward = trew[0]
        for d in range(1, n):
            total_reward = total_reward + trew[d]
        mean = total_reward / n
        squares = jnp.zeros((8, 128), F32)
        for d in range(n):
            squares = squares + (trew[d] - mean) * (trew[d] - mean)
        gsum[grp] = squares
        pltpu.make_async_copy(tinfo, tsm, sm_sem).start()
        for i in range(1, groups):
            group_copy(i).start()
        return mean

    live = lax.broadcasted_iota(jnp.int32, (rows, width), 0) < rlen[0, 0]

    def combine_head(h, owner, c, j, piece_of):
        right = jnp.broadcast_to(ptot32[pl.ds(h, 1), :], (width, 2 * feat)).astype(BF16)
        prompt = dot(phq[h], jnp.concatenate([state[owner, c, lines(j), :], right], axis=0), NT)
        both = prompt.astype(BF16).astype(F32) + inum[h]
        result = jnp.where(live, both[:, :width] / both[:, width:], 0.0)
        cols = pl.ds(pl.multiple_of(h * width, 128), width)
        for i in range(n):
            block = result[:BLK]
            for p in range(1, pieces):
                block = jnp.where(piece_of[i] == p, result[p * BLK : (p + 1) * BLK], block)
            ostage[i, :, cols] = block.astype(BF16)

    def combine(c, piece_of):
        for step in range(1, n):
            if step not in feeds(c):
                state_copy(c, step).wait_recv()

        def body(t, carry):
            owner, j = t // per, t % per
            combine_head(owner * own + c * per + j, owner, c, j, piece_of)
            return carry

        lax.fori_loop(0, n * per, body, 0)
        for g in range(n):
            for i in [*range(1, n), 0]:
                out_copy(c, g, i).start()

    for copy in loads[:3]:
        copy.wait()
    partial_states(0)
    pl.semaphore_wait(barrier, n + groups - 2)
    start_first(0)
    for i in range(1, n):
        for copy in info_copies(i):
            copy.start()
    for c in range(1, chunks):
        partial_states(c)
        start_first(c)
    ptot[me] = ptot32[...].astype(BF16)
    for i in range(1, n):
        total_copy(i).start()
    for copy in loads[3:]:
        copy.wait()

    def share(part_of):
        return heads * part_of // 32 // 2 * 2

    half = -(-chunks // 2)
    intra(0, share(4))
    for c in range(half):
        pass_on(c)
    intra(share(4), share(10))
    for c in range(half, chunks):
        pass_on(c)
    mean = rewards_and_tables()
    for c in range(half):
        settle(c)
    intra(share(10), share(16))
    for c in range(half, chunks):
        settle(c)
    for c in range(half):
        relay(c)
    intra(share(16), share(24))
    for c in range(half, chunks):
        relay(c)
    pltpu.make_async_copy(tinfo, tsm, sm_sem).wait()
    for i in range(1, n):
        total_copy(i).wait_recv()
    totals = ptot[0].astype(F32)
    for d in range(1, n):
        totals = totals + ptot[d].astype(F32)
    ptot32[...] = totals
    piece_of = []
    for i in range(n):
        found = jnp.int32(0)
        for j in range(slot_count):
            ident = tsm[peer(i), 0, j] - me * pieces
            found = jnp.where((ident >= 0) & (ident < pieces), ident, found)
        piece_of.append(found)
    for c in range(chunks):
        if c == chunks // 2:
            intra(share(24), heads)
        combine(c, piece_of)
    for i in range(1, groups):
        group_copy(i).wait_recv()
    spread = gsum[0]
    for g in range(1, groups):
        spread = spread + gsum[g]
    scale = jnp.sqrt(spread / (groups * n) + 1e-06)
    adv = jnp.zeros((8, 128), F32)
    for j in range(slot_count):
        ident = slots_sm[0, j]
        src = lax.div(ident, pieces)
        start = lax.rem(ident, pieces) * BLK
        reward = jnp.zeros((8, 128), F32)
        size = jnp.int32(0)
        for d in range(n):
            reward = jnp.where(src == d, trew[d], reward)
            size = jnp.where(src == d, tsm[d, 0, slot_count], size)
        value = jnp.where(start + lane - j * BLK < size, (reward - mean) / scale, 0.0)
        adv = jnp.where((lane >= j * BLK) & (lane < (j + 1) * BLK), value, adv)
    adv_ref[...] = adv[:1]

    for i in range(1, n):
        for copy in info_copies(i):
            copy.wait_send()
        total_copy(i).wait_send()
    for c in range(chunks):
        for i in range(1, sizes(c)[0]):
            first_copy(c, i).wait_send()
        for i in range(1, sizes(c)[1]):
            second_copy(c, i).wait_send()
        for i in range(1, n):
            state_copy(c, i).wait_send()
    for i in range(1, groups):
        group_copy(i).wait_send()
    for c in range(chunks):
        for g in range(n):
            for i in range(n):
                out_copy(c, g, i).wait()


def pick(slots, block_ref, adv_ref, out_ref, adv_out_ref):
    out_ref[...] = block_ref[...]
    adv_out_ref[...] = adv_ref[...]


def body(
    resp_q, resp_k, resp_v, prompt_k, prompt_v, prompt_len, resp_len, assign, rewards,
    feat_q, feat_k,
):
    n = lax.axis_size("dp")
    groups = lax.axis_size("group")
    heads, width, feat = feat_q.shape
    rows = resp_q.shape[1]
    prows = prompt_k.shape[1]
    model = resp_q.shape[2]
    own = heads // n
    chunks = next(c for c in (4, 2, 1) if own % c == 0)
    per = own // chunks
    slot_count = assign.shape[1]
    smem = pl.BlockSpec(memory_space=pltpu.SMEM)
    hbm = pl.BlockSpec(memory_space=pl.ANY)
    vmem = pl.BlockSpec(memory_space=pltpu.VMEM)
    dma = pltpu.SemaphoreType.DMA
    across = max(b for b in range(1, n + 1) if n % b == 0 and b * b <= n)
    most = max(across, n // across)
    others = max(most - 1, 1)
    entry = (per * width, 2 * feat)
    arrived, adv = pl.pallas_call(
        functools.partial(kernel, n, across, groups, heads, chunks),
        out_shape=(
            jax.ShapeDtypeStruct((n, BLK, model), BF16),
            jax.ShapeDtypeStruct((1, slot_count * BLK), F32),
        ),
        in_specs=[smem] * 4 + [hbm] * 7,
        out_specs=(hbm, vmem),
        scratch_shapes=[
            pltpu.VMEM((rows, model), BF16),
            pltpu.VMEM((rows, model), BF16),
            pltpu.VMEM((rows, model), BF16),
            pltpu.VMEM((heads, width, feat), BF16),
            pltpu.VMEM((heads, width, feat), BF16),
            pltpu.VMEM((prows, model), BF16),
            pltpu.VMEM((prows, model), BF16),
            pltpu.VMEM((chunks, most, most, *entry), BF16),
            pltpu.VMEM((chunks, others, most, *entry), BF16),
            pltpu.VMEM((chunks, others, *entry), BF16),
            pltpu.VMEM((chunks, others, *entry), BF16),
            pltpu.VMEM((n, chunks, *entry), BF16),
            pltpu.VMEM((heads, 2 * feat), F32),
            pltpu.VMEM((n, heads, 2 * feat), BF16),
            pltpu.VMEM((heads, rows, 2 * feat), BF16),
            pltpu.VMEM((heads, rows, 2 * width), F32),
            pltpu.VMEM((n, BLK, model), BF16),
            pltpu.VMEM((n, 8, 128), jnp.int32),
            pltpu.VMEM((n, 8, 128), F32),
            pltpu.SMEM((n, 8, 128), jnp.int32),
            pltpu.VMEM((groups, 8, 128), F32),
            dma((7,)),
            dma((chunks, n)),
            dma((chunks, most)),
            dma((chunks, most)),
            dma((chunks, most)),
            dma((chunks, most)),
            dma((n,)),
            dma((n,)),
            dma((chunks, n)),
            dma((chunks, n)),
            dma((chunks, n, n)),
            dma((chunks, n, n)),
            dma((2, n)),
            dma((2, n)),
            dma((groups,)),
            dma((groups,)),
            dma,
        ],
        compiler_params=pltpu.CompilerParams(
            collective_id=0, has_side_effects=True, vmem_limit_bytes=62 * 1024 * 1024
        ),
        name="hedgehog",
    )(
        prompt_len, resp_len, assign, rewards, resp_q, resp_k, resp_v, prompt_k, prompt_v,
        feat_q, feat_k,
    )

    pieces = rows // BLK
    return pl.pallas_call(
        pick,
        out_shape=(
            jax.ShapeDtypeStruct((1, slot_count * BLK, model), BF16),
            jax.ShapeDtypeStruct(adv.shape, F32),
        ),
        grid_spec=pltpu.PrefetchScalarGridSpec(
            num_scalar_prefetch=1,
            grid=(slot_count,),
            in_specs=[
                pl.BlockSpec((1, BLK, model), lambda j, slots: (lax.div(slots[0, j], pieces), 0, 0)),
                pl.BlockSpec(adv.shape, lambda j, slots: (0, 0)),
            ],
            out_specs=(
                pl.BlockSpec((1, BLK, model), lambda j, slots: (0, j, 0)),
                pl.BlockSpec(adv.shape, lambda j, slots: (0, 0)),
            ),
        ),
        name="pick",
    )(assign, arrived, adv)


def solution(mesh):
    return jax.shard_map(
        body,
        mesh=mesh,
        in_specs=(
            P("group", "dp", None),
            P("group", "dp", None),
            P("group", "dp", None),
            P("group", "dp", None),
            P("group", "dp", None),
            P("group"),
            P("group", "dp"),
            P("group", "dp"),
            P("group", "dp"),
            P(),
            P(),
        ),
        out_specs=(P("group", "dp", None), P("group", "dp")),
        check_vma=False,
    )
```

```python
import functools

import jax
import jax.numpy as jnp
from jax import lax
from jax.experimental import pallas as pl
from jax.experimental.pallas import tpu as pltpu
from jax.sharding import PartitionSpec as P

BLK = 64
MESH = pl.DeviceIdType.MESH
NT = (((1,), (1,)), ((), ()))
NN = (((1,), (0,)), ((), ()))
F32 = jnp.float32
BF16 = jnp.bfloat16
LOG2E = 1.4426950408889634
EXTRA = 16


def dot(a, b, dims=NN):
    return lax.dot_general(a, b, dims, preferred_element_type=F32)


def features(rows, weights):
    logits = [dot(w.T, x, NT) for x, w in zip(rows, weights)]
    tops = [jnp.max(u, axis=0, keepdims=True) for u in logits]
    lows = [jnp.min(u, axis=0, keepdims=True) for u in logits]
    ups = [jnp.exp2((u - top) * LOG2E) for u, top in zip(logits, tops)]
    downs = [jnp.exp2((low - u) * LOG2E) for u, low in zip(logits, lows)]
    up_scales = [1.0 / jnp.sum(e, axis=0, keepdims=True) for e in ups]
    down_scales = [1.0 / jnp.sum(e, axis=0, keepdims=True) for e in downs]
    return [
        jnp.concatenate([(a * r).astype(BF16), (b * q).astype(BF16)], axis=0)
        for a, b, r, q in zip(ups, downs, up_scales, down_scales)
    ]


def kernel(
    n, across, groups, heads, chunks,
    plen_hbm, rlen_hbm, slots_hbm, rew_hbm, q_hbm, k_hbm, v_hbm, pk_hbm, pv_hbm, fq_hbm, fk_hbm,
    orecv, adv_ref,
    qs, ks, vs, fqs, fks, pks, pvs, part, first_in, passing, second_in, state,
    ptot32, ptot, phq, inum, ostage,
    plen, rlen, slots_sm, rew_sm, tinfo, trew, tsm, gsum, spread_all,
    load_sem, oself_sem, a_send, a_recv, b_send, b_recv, t_send, t_recv,
    st_send, st_recv, o_send, o_recv,
    i_send, i_recv, g_send, g_recv, s_send, s_recv, sm_sem, small_sem, entry_sem,
):
    me = lax.axis_index("dp")
    grp = lax.axis_index("group")
    rows = qs.shape[0]
    width = fqs.shape[1]
    feat = fqs.shape[2]
    pieces = rows // BLK
    slot_count = slots_hbm.shape[1]
    own = heads // n
    per = own // chunks
    prows = pks.shape[0]

    down = n // across
    row = me // across
    col = me % across

    def peer(i):
        return (row + i // across) % down * across + (col + i % across) % across

    def source(i):
        return (row + down - i // across) % down * across + (col + across - i % across) % across

    span = n * per

    def loads(c, pairs):
        cols = pl.ds(c * span * width, span * width)
        at = pl.ds(c * span, span)
        result = []
        for hbm, buf in pairs:
            if len(buf.shape) == 3:
                src, dst = hbm.at[at], buf.at[at]
            else:
                src, dst = hbm.at[0, :, cols], buf.at[:, cols]
            result.append((src, dst))
        return result

    def prompt_loads(c):
        ends = loads(c, [(fk_hbm, fks), (pk_hbm, pks), (pv_hbm, pvs)])
        return [
            pltpu.make_async_copy(src, dst, load_sem.at[c, i]) for i, (src, dst) in enumerate(ends)
        ]

    def resp_loads(c):
        ends = loads(c, [(fq_hbm, fqs), (q_hbm, qs), (k_hbm, ks), (v_hbm, vs)])
        return [
            pltpu.make_async_copy(src, dst, load_sem.at[c, 3 + i])
            for i, (src, dst) in enumerate(ends)
        ]

    small = [
        pltpu.make_async_copy(src, dst, small_sem.at[i])
        for i, (src, dst) in enumerate(
            [(plen_hbm, plen), (rlen_hbm, rlen), (slots_hbm, slots_sm), (rew_hbm, rew_sm)]
        )
    ]
    barrier = pltpu.get_barrier_semaphore()
    for i in range(1, n):

        @pl.when(peer(i) != 0)
        def _(i=i):
            pl.semaphore_signal(barrier, inc=1, device_id={"dp": peer(i)}, device_id_type=MESH)

    @pl.when(me == 0)
    def _():
        for i in range(1, groups):
            pl.semaphore_signal(
                barrier, inc=1, device_id={"group": lax.rem(grp + i, groups)}, device_id_type=MESH
            )

    for copy in prompt_loads(0) + small + prompt_loads(min(1, chunks - 1))[: 3 * (chunks > 1)]:
        copy.start()

    @pl.when(me != 0)
    def _():
        pl.semaphore_wait(barrier, n - 1)
        pl.semaphore_signal(entry_sem, inc=1, device_id={"dp": 0}, device_id_type=MESH)

    for copy in small:
        copy.wait()
    lane = lax.broadcasted_iota(jnp.int32, (8, 128), 1)
    info = jnp.where(lane == slot_count, rlen[0, 0], 0)
    for j in range(slot_count):
        info = jnp.where(lane == j, slots_sm[0, j], info)
    tinfo[me] = info
    trew[me] = jnp.full((8, 128), rew_sm[0, 0], F32)

    def remote(src, dst, send, recv, axis, target):
        return pltpu.make_async_remote_copy(
            src_ref=src, dst_ref=dst, send_sem=send, recv_sem=recv,
            device_id={axis: target}, device_id_type=MESH,
        )

    def info_copies(i):
        return [
            remote(tinfo.at[me], tinfo.at[me], i_send.at[0, i], i_recv.at[0, i], "dp", peer(i)),
            remote(trew.at[me], trew.at[me], i_send.at[1, i], i_recv.at[1, i], "dp", peer(i)),
        ]

    def group_copy(i):
        return remote(
            gsum.at[grp], gsum.at[grp], g_send.at[i], g_recv.at[i], "group",
            lax.rem(grp + i, groups),
        )

    def total_copy(i):
        return remote(ptot.at[me], ptot.at[me], t_send.at[i], t_recv.at[i], "dp", peer(i))

    def sizes(c):
        return (across, down) if c % 2 == 0 else (down, across)

    def offset(c, one, two):
        return two * across + one if c % 2 == 0 else one * across + two

    def first_copy(c, i):
        span = pl.ds(0, sizes(c)[1])
        return remote(
            part.at[c, i, span], first_in.at[c, i - 1, span], a_send.at[c, i], a_recv.at[c, i],
            "dp", peer(offset(c, i, 0)),
        )

    def second_copy(c, i):
        return remote(
            passing.at[c, i - 1], second_in.at[c, i - 1], b_send.at[c, i], b_recv.at[c, i],
            "dp", peer(offset(c, 0, i)),
        )

    def state_copy(c, i):
        dr, dc = i // across, i % across
        if c % 2 == 0:
            target, holder = (dr * across, dc) if dr else (dc, 0)
        else:
            target, holder = (dc, dr * across) if dc else (dr * across, 0)
        chunk = state.at[source(holder), c]
        return remote(chunk, chunk, st_send.at[c, i], st_recv.at[c, i], "dp", peer(target))

    straight = [i for i in range(1, n) if i < across or i % across == 0]
    relayed = [i for i in range(1, n) if i not in straight]

    def feeds(c):
        return [i for i in straight if (i < across if c % 2 == 0 else i % across == 0)]

    def relay(c):
        for i in feeds(c):
            state_copy(c, i).wait_recv()
        for i in relayed:
            state_copy(c, i).start()

    def out_copy(c, i):
        src, dst = ostage.at[c, i], orecv.at[me, c]
        if i == 0:
            return pltpu.make_async_copy(src, dst, oself_sem.at[c])
        return remote(src, dst, o_send.at[c, i], o_recv.at[c, i], "dp", peer(i))

    def lines(j):
        return pl.ds(pl.multiple_of(j * width, 128), width)

    def batches(count, limit, act):
        size = next(b for b in range(min(limit, count), 0, -1) if count % b == 0)

        def step(t, carry):
            act([t * size + u for u in range(size)])
            return carry

        if count == size:
            act(list(range(size)))
        else:
            lax.fori_loop(0, count // size, step, 0)

    keep = lax.broadcasted_iota(jnp.int32, (width + EXTRA, prows), 1) + me * prows < plen[0]

    def partial_states(c, mine):
        one_size, two_size = sizes(c)
        if one_size == 1 and not mine:
            return

        def act(places):
            spots = []
            for p in places:
                one = 0 if mine else p // (per * two_size) + 1
                two, j = p // per % two_size, p % per
                h = c * span + peer(offset(c, one, two)) * per + j
                spots.append((one, two, j, h))
            keys = features(
                [pks[:, lines(h)] for *_, h in spots], [fks[h] for *_, h in spots]
            )
            values = [
                jnp.concatenate([pvs[:, lines(h)].T, jnp.ones((EXTRA, prows), BF16)], axis=0)
                for *_, h in spots
            ]
            values = [jnp.where(keep, v.astype(F32), 0.0).astype(BF16) for v in values]
            found = [dot(v, k, NT) for v, k in zip(values, keys)]
            for (one, two, j, h), f in zip(spots, found):
                part[c, one, two, lines(j), :] = f[:width].astype(BF16)
                ptot32[pl.ds(h, 1), :] = f[width : width + 1]

        batches(two_size * per * (1 if mine else one_size - 1), 4, act)

    def start_first(c):
        for i in range(1, sizes(c)[0]):
            first_copy(c, i).start()

    def pass_on(c):
        one_size, two_size = sizes(c)
        for i in range(1, one_size):
            first_copy(c, i).wait_recv()
        for two in range(1, two_size):

            def step(j, carry, two=two):
                total = part[c, 0, two, lines(j), :].astype(F32)
                for i in range(1, one_size):
                    total = total + first_in[c, i - 1, two, lines(j), :].astype(F32)
                passing[c, two - 1, lines(j), :] = total.astype(BF16)
                return carry

            lax.fori_loop(0, per, step, 0)
            second_copy(c, two).start()

    def settle(c):
        one_size, two_size = sizes(c)
        for i in range(1, two_size):
            second_copy(c, i).wait_recv()

        def step(j, carry):
            total = part[c, 0, 0, lines(j), :].astype(F32)
            for i in range(1, one_size):
                total = total + first_in[c, i - 1, 0, lines(j), :].astype(F32)
            for i in range(1, two_size):
                total = total + second_in[c, i - 1, lines(j), :].astype(F32)
            state[me, c, lines(j), :] = total.astype(BF16)
            return carry

        lax.fori_loop(0, per, step, 0)
        for i in straight:
            state_copy(c, i).start()

    causal = lax.broadcasted_iota(jnp.int32, (rows, rows), 0) <= lax.broadcasted_iota(
        jnp.int32, (rows, rows), 1
    )

    def intra(begin, end):
        def act(places):
            heads_here = [begin + p for p in places]
            cols = [lines(h) for h in heads_here]
            qf = features([qs[:, i] for i in cols], [fqs[h] for h in heads_here])
            for h, q in zip(heads_here, qf):
                phq[h] = q
            kf = [k.T for k in features([ks[:, i] for i in cols], [fks[h] for h in heads_here])]
            values = [
                jnp.concatenate([vs[:, i].T, jnp.ones((EXTRA, rows), BF16)], axis=0) for i in cols
            ]
            scores = [dot(k, q) for k, q in zip(kf, qf)]
            weights = [jnp.where(causal, x, 0.0).astype(BF16) for x in scores]
            found = [dot(v, w) for v, w in zip(values, weights)]
            for h, f in zip(heads_here, found):
                inum[h] = f

        if end > begin:
            batches(end - begin, 4, act)

    def rewards_and_tables():
        for i in range(1, n):
            for copy in info_copies(i):
                copy.wait_recv()
        total_reward = trew[0]
        for d in range(1, n):
            total_reward = total_reward + trew[d]
        mean = total_reward / n
        squares = jnp.zeros((8, 128), F32)
        for d in range(n):
            squares = squares + (trew[d] - mean) * (trew[d] - mean)
        gsum[grp] = squares
        pltpu.make_async_copy(tinfo, tsm, sm_sem).start()
        return mean

    def spread_copy(i):
        return remote(spread_all, spread_all, s_send.at[i], s_recv, "dp", peer(i))

    def squares_out():
        @pl.when(me == 0)
        def _():
            pl.semaphore_wait(barrier, groups - 1)
            for i in range(1, groups):
                group_copy(i).start()

    def squares_in():
        @pl.when(me == 0)
        def _():
            for i in range(1, groups):
                group_copy(i).wait_recv()
            spread = gsum[0]
            for g in range(1, groups):
                spread = spread + gsum[g]
            spread_all[...] = spread
            for i in range(1, n):
                spread_copy(i).start()

    live = lax.broadcasted_iota(jnp.int32, (1, rows), 1) < rlen[0, 0]

    def combine(c, piece_of):
        for step in range(1, n):
            if step not in feeds(c):
                state_copy(c, step).wait_recv()

        def act(places):
            spots = []
            for p in places:
                owner, j = p // per, p % per
                spots.append((p, owner, j, c * span + p))
            totals = [
                jnp.broadcast_to(ptot32[pl.ds(h, 1), :], (EXTRA, 2 * feat)).astype(BF16)
                for *_, h in spots
            ]
            prompts = [
                dot(jnp.concatenate([state[owner, c, lines(j), :], total], axis=0), phq[h])
                for (_, owner, j, h), total in zip(spots, totals)
            ]
            both = [x.astype(BF16).astype(F32) + inum[h] for (*_, h), x in zip(spots, prompts)]
            scales = [jnp.where(live, 1.0 / b[width : width + 1], 0.0) for b in both]
            results = [(b[:width] * r).astype(BF16).T for b, r in zip(both, scales)]
            for (p, *_), result in zip(spots, results):
                for i in range(n):
                    block = result[:BLK]
                    for q in range(1, pieces):
                        block = jnp.where(
                            piece_of[i] == q, result[q * BLK : (q + 1) * BLK], block
                        )
                    ostage[c, i, :, lines(p)] = block

        batches(n * per, 8, act)
        for i in [*range(1, n), 0]:
            out_copy(c, i).start()

    def entered():
        @pl.when(me == 0)
        def _():
            pl.semaphore_wait(entry_sem, n - 1)

    for begin in range(0, chunks, 2):
        here = range(begin, min(begin + 2, chunks))
        for c in here:
            for copy in prompt_loads(c):
                copy.wait()
            if c + 2 < chunks:
                for copy in prompt_loads(c + 2):
                    copy.start()
            partial_states(c, False)
            if c == 0:
                entered()
            start_first(c)
        for c in here:
            for copy in resp_loads(c):
                copy.start()
        for c in here:
            partial_states(c, True)
        if begin == 0:
            for i in range(1, n):
                for copy in info_copies(i):
                    copy.start()
    ptot[me] = ptot32[...].astype(BF16)
    for i in range(1, n):
        total_copy(i).start()
    for c in range(chunks):
        for copy in resp_loads(c):
            copy.wait()

    def share(part_of):
        return heads * part_of // 32 // 2 * 2

    half = -(-chunks // 2)
    intra(0, share(8))
    for c in range(half):
        pass_on(c)
    intra(share(8), share(16))
    for c in range(half, chunks):
        pass_on(c)
    mean = rewards_and_tables()
    for c in range(half):
        settle(c)
    intra(share(16), share(24))
    for c in range(half, chunks):
        settle(c)
    for c in range(half):
        relay(c)
    intra(share(24), heads)
    squares_out()
    for c in range(half, chunks):
        relay(c)
    pltpu.make_async_copy(tinfo, tsm, sm_sem).wait()
    for i in range(1, n):
        total_copy(i).wait_recv()
    totals = ptot[0].astype(F32)
    for d in range(1, n):
        totals = totals + ptot[d].astype(F32)
    ptot32[...] = totals
    piece_of = []
    for i in range(n):
        found = jnp.int32(0)
        for j in range(slot_count):
            ident = tsm[peer(i), 0, j] - me * pieces
            found = jnp.where((ident >= 0) & (ident < pieces), ident, found)
        piece_of.append(found)
    for c in range(chunks):
        combine(c, piece_of)
    squares_in()

    @pl.when(me != 0)
    def _():
        spread_copy(1).wait_recv()

    scale = jnp.sqrt(spread_all[...] / (groups * n) + 1e-06)
    adv = jnp.zeros((8, 128), F32)
    for j in range(slot_count):
        ident = slots_sm[0, j]
        src = lax.div(ident, pieces)
        start = lax.rem(ident, pieces) * BLK
        reward = jnp.zeros((8, 128), F32)
        size = jnp.int32(0)
        for d in range(n):
            reward = jnp.where(src == d, trew[d], reward)
            size = jnp.where(src == d, tsm[d, 0, slot_count], size)
        value = jnp.where(start + lane - j * BLK < size, (reward - mean) / scale, 0.0)
        adv = jnp.where((lane >= j * BLK) & (lane < (j + 1) * BLK), value, adv)
    adv_ref[...] = adv[:1]

    for i in range(1, n):
        for copy in info_copies(i):
            copy.wait_send()
        total_copy(i).wait_send()
    for c in range(chunks):
        for i in range(1, sizes(c)[0]):
            first_copy(c, i).wait_send()
        for i in range(1, sizes(c)[1]):
            second_copy(c, i).wait_send()
        for i in range(1, n):
            state_copy(c, i).wait_send()

    @pl.when(me == 0)
    def _():
        for i in range(1, groups):
            group_copy(i).wait_send()
        for i in range(1, n):
            spread_copy(i).wait_send()

    for c in range(chunks):
        for i in range(n):
            out_copy(c, i).wait()


def pick(slots, plen, rlen, rew, block_ref, adv_ref, out_ref, adv_out_ref):
    chunks, span = block_ref.shape[1], block_ref.shape[3]
    for c in range(chunks):
        out_ref[0, :, c * span : (c + 1) * span] = block_ref[0, c]
    adv_out_ref[...] = adv_ref[...]


def body(
    resp_q, resp_k, resp_v, prompt_k, prompt_v, prompt_len, resp_len, assign, rewards,
    feat_q, feat_k,
):
    n = lax.axis_size("dp")
    groups = lax.axis_size("group")
    heads, width, feat = feat_q.shape
    rows = resp_q.shape[1]
    prows = prompt_k.shape[1]
    model = resp_q.shape[2]
    own = heads // n
    chunks = next(c for c in (4, 2, 1) if own % c == 0)
    per = own // chunks
    slot_count = assign.shape[1]
    hbm = pl.BlockSpec(memory_space=pltpu.HBM)
    vmem = pl.BlockSpec(memory_space=pltpu.VMEM)
    dma = pltpu.SemaphoreType.DMA
    across = max(b for b in range(1, n + 1) if n % b == 0 and b * b <= n)
    most = max(across, n // across)
    others = max(most - 1, 1)
    entry = (per * width, 2 * feat)
    arrived, adv = pl.pallas_call(
        functools.partial(kernel, n, across, groups, heads, chunks),
        out_shape=(
            jax.ShapeDtypeStruct((n, chunks, BLK, model // chunks), BF16),
            jax.ShapeDtypeStruct((1, slot_count * BLK), F32),
        ),
        in_specs=[hbm] * 11,
        out_specs=(hbm, vmem),
        scratch_shapes=[
            pltpu.VMEM((rows, model), BF16),
            pltpu.VMEM((rows, model), BF16),
            pltpu.VMEM((rows, model), BF16),
            pltpu.VMEM((heads, width, feat), BF16),
            pltpu.VMEM((heads, width, feat), BF16),
            pltpu.VMEM((prows, model), BF16),
            pltpu.VMEM((prows, model), BF16),
            pltpu.VMEM((chunks, most, most, *entry), BF16),
            pltpu.VMEM((chunks, others, most, *entry), BF16),
            pltpu.VMEM((chunks, others, *entry), BF16),
            pltpu.VMEM((chunks, others, *entry), BF16),
            pltpu.VMEM((n, chunks, *entry), BF16),
            pltpu.VMEM((heads, 2 * feat), F32),
            pltpu.VMEM((n, heads, 2 * feat), BF16),
            pltpu.VMEM((heads, 2 * feat, rows), BF16),
            pltpu.VMEM((heads, width + EXTRA, rows), F32),
            pltpu.VMEM((chunks, n, BLK, model // chunks), BF16),
            pltpu.SMEM(prompt_len.shape, jnp.int32),
            pltpu.SMEM(resp_len.shape, jnp.int32),
            pltpu.SMEM(assign.shape, jnp.int32),
            pltpu.SMEM(rewards.shape, F32),
            pltpu.VMEM((n, 8, 128), jnp.int32),
            pltpu.VMEM((n, 8, 128), F32),
            pltpu.SMEM((n, 8, 128), jnp.int32),
            pltpu.VMEM((groups, 8, 128), F32),
            pltpu.VMEM((8, 128), F32),
            dma((chunks, 7)),
            dma((chunks,)),
            dma((chunks, most)),
            dma((chunks, most)),
            dma((chunks, most)),
            dma((chunks, most)),
            dma((n,)),
            dma((n,)),
            dma((chunks, n)),
            dma((chunks, n)),
            dma((chunks, n)),
            dma((chunks, n)),
            dma((2, n)),
            dma((2, n)),
            dma((groups,)),
            dma((groups,)),
            dma((n,)),
            dma,
            dma,
            dma((4,)),
            pltpu.SemaphoreType.REGULAR,
        ],
        compiler_params=pltpu.CompilerParams(
            collective_id=0, has_side_effects=True, vmem_limit_bytes=62 * 1024 * 1024
        ),
        name="hedgehog",
    )(
        prompt_len, resp_len, assign, rewards, resp_q, resp_k, resp_v, prompt_k, prompt_v,
        feat_q, feat_k,
    )

    pieces = rows // BLK
    return pl.pallas_call(
        pick,
        out_shape=(
            jax.ShapeDtypeStruct((1, slot_count * BLK, model), BF16),
            jax.ShapeDtypeStruct(adv.shape, F32),
        ),
        grid_spec=pltpu.PrefetchScalarGridSpec(
            num_scalar_prefetch=4,
            grid=(slot_count,),
            in_specs=[
                pl.BlockSpec(
                    (1, chunks, BLK, model // chunks),
                    lambda j, slots, *_: (lax.div(slots[0, j], pieces), 0, 0, 0),
                ),
                pl.BlockSpec(adv.shape, lambda j, slots, *_: (0, 0)),
            ],
            out_specs=(
                pl.BlockSpec((1, BLK, model), lambda j, slots, *_: (0, j, 0)),
                pl.BlockSpec(adv.shape, lambda j, slots, *_: (0, 0)),
            ),
        ),
        name="pick",
    )(assign, prompt_len, resp_len, rewards, arrived, adv)


def solution(mesh):
    return jax.shard_map(
        body,
        mesh=mesh,
        in_specs=(
            P("group", "dp", None),
            P("group", "dp", None),
            P("group", "dp", None),
            P("group", "dp", None),
            P("group", "dp", None),
            P("group"),
            P("group", "dp"),
            P("group", "dp"),
            P("group", "dp"),
            P(),
            P(),
        ),
        out_specs=(P("group", "dp", None), P("group", "dp")),
        check_vma=False,
    )
```

```python
import functools

import jax
import jax.numpy as jnp
from jax import lax
from jax.experimental import pallas as pl
from jax.experimental.pallas import tpu as pltpu
from jax.sharding import PartitionSpec as P

BLK = 64
MESH = pl.DeviceIdType.MESH
NT = (((1,), (1,)), ((), ()))
NN = (((1,), (0,)), ((), ()))
F32 = jnp.float32
BF16 = jnp.bfloat16
LOG2E = 1.4426950408889634
EXTRA = 16


def dot(a, b, dims=NN):
    return lax.dot_general(a, b, dims, preferred_element_type=F32)


def features(rows, weights):
    logits = [dot(w.T, x, NT) for x, w in zip(rows, weights)]
    tops = [jnp.max(u, axis=0, keepdims=True) for u in logits]
    lows = [jnp.min(u, axis=0, keepdims=True) for u in logits]
    ups = [jnp.exp2((u - top) * LOG2E) for u, top in zip(logits, tops)]
    downs = [jnp.exp2((low - u) * LOG2E) for u, low in zip(logits, lows)]
    up_scales = [1.0 / jnp.sum(e, axis=0, keepdims=True) for e in ups]
    down_scales = [1.0 / jnp.sum(e, axis=0, keepdims=True) for e in downs]
    return [
        jnp.concatenate([(a * r).astype(BF16), (b * q).astype(BF16)], axis=0)
        for a, b, r, q in zip(ups, downs, up_scales, down_scales)
    ]


def kernel(
    n, across, groups, heads, chunks,
    plen_hbm, rlen_hbm, slots_hbm, rew_hbm, q_hbm, k_hbm, v_hbm, pk_hbm, pv_hbm, fq_hbm, fk_hbm,
    orecv, adv_ref,
    qs, ks, vs, fqs, fks, pks, pvs, part, first_in, passing, second_in, state,
    ptot32, ptot, phq, inum, ostage,
    plen, rlen, slots_sm, rew_sm, tinfo, trew, tsm, gsum, spread_all,
    load_sem, oself_sem, a_send, a_recv, b_send, b_recv, t_send, t_recv,
    st_send, st_recv, o_send, o_recv,
    i_send, i_recv, g_send, g_recv, s_send, s_recv, sm_sem, small_sem, entry_sem,
):
    me = lax.axis_index("dp")
    grp = lax.axis_index("group")
    rows = qs.shape[0]
    width = fqs.shape[1]
    feat = fqs.shape[2]
    pieces = rows // BLK
    slot_count = slots_hbm.shape[1]
    own = heads // n
    per = own // chunks
    prows = pks.shape[0]

    down = n // across
    row = me // across
    col = me % across

    def peer(i):
        return (row + i // across) % down * across + (col + i % across) % across

    def source(i):
        return (row + down - i // across) % down * across + (col + across - i % across) % across

    span = n * per

    def loads(c, pairs):
        cols = pl.ds(c * span * width, span * width)
        at = pl.ds(c * span, span)
        result = []
        for hbm, buf in pairs:
            if len(buf.shape) == 3:
                src, dst = hbm.at[at], buf.at[at]
            else:
                src, dst = hbm.at[0, :, cols], buf.at[:, cols]
            result.append((src, dst))
        return result

    def prompt_loads(c):
        ends = loads(c, [(fk_hbm, fks), (pk_hbm, pks), (pv_hbm, pvs)])
        return [
            pltpu.make_async_copy(src, dst, load_sem.at[c, i]) for i, (src, dst) in enumerate(ends)
        ]

    def resp_loads(c):
        ends = loads(c, [(fq_hbm, fqs), (q_hbm, qs), (k_hbm, ks), (v_hbm, vs)])
        return [
            pltpu.make_async_copy(src, dst, load_sem.at[c, 3 + i])
            for i, (src, dst) in enumerate(ends)
        ]

    small = [
        pltpu.make_async_copy(src, dst, small_sem.at[i])
        for i, (src, dst) in enumerate(
            [(plen_hbm, plen), (rlen_hbm, rlen), (slots_hbm, slots_sm), (rew_hbm, rew_sm)]
        )
    ]
    barrier = pltpu.get_barrier_semaphore()
    for i in range(1, n):

        @pl.when(peer(i) != 0)
        def _(i=i):
            pl.semaphore_signal(barrier, inc=1, device_id={"dp": peer(i)}, device_id_type=MESH)

    @pl.when(me == 0)
    def _():
        for i in range(1, groups):
            pl.semaphore_signal(
                barrier, inc=1, device_id={"group": lax.rem(grp + i, groups)}, device_id_type=MESH
            )

    for copy in prompt_loads(0) + small + prompt_loads(min(1, chunks - 1))[: 3 * (chunks > 1)]:
        copy.start()

    @pl.when(me != 0)
    def _():
        pl.semaphore_wait(barrier, n - 1)
        pl.semaphore_signal(entry_sem, inc=1, device_id={"dp": 0}, device_id_type=MESH)

    for copy in small:
        copy.wait()
    lane = lax.broadcasted_iota(jnp.int32, (8, 128), 1)
    info = jnp.where(lane == slot_count, rlen[0, 0], 0)
    for j in range(slot_count):
        info = jnp.where(lane == j, slots_sm[0, j], info)
    tinfo[me] = info
    trew[me] = jnp.full((8, 128), rew_sm[0, 0], F32)

    def remote(src, dst, send, recv, axis, target):
        return pltpu.make_async_remote_copy(
            src_ref=src, dst_ref=dst, send_sem=send, recv_sem=recv,
            device_id={axis: target}, device_id_type=MESH,
        )

    def info_copies(i):
        return [
            remote(tinfo.at[me], tinfo.at[me], i_send.at[0, i], i_recv.at[0, i], "dp", peer(i)),
            remote(trew.at[me], trew.at[me], i_send.at[1, i], i_recv.at[1, i], "dp", peer(i)),
        ]

    def group_copy(i):
        return remote(
            gsum.at[grp], gsum.at[grp], g_send.at[i], g_recv.at[i], "group",
            lax.rem(grp + i, groups),
        )

    def total_copy(i):
        return remote(ptot.at[me], ptot.at[me], t_send.at[i], t_recv.at[i], "dp", peer(i))

    def sizes(c):
        return (across, down) if c % 2 == 0 else (down, across)

    def offset(c, one, two):
        return two * across + one if c % 2 == 0 else one * across + two

    def first_copy(c, i):
        span = pl.ds(0, sizes(c)[1])
        return remote(
            part.at[c, i, span], first_in.at[c, i - 1, span], a_send.at[c, i], a_recv.at[c, i],
            "dp", peer(offset(c, i, 0)),
        )

    def second_copy(c, i):
        return remote(
            passing.at[c, i - 1], second_in.at[c, i - 1], b_send.at[c, i], b_recv.at[c, i],
            "dp", peer(offset(c, 0, i)),
        )

    def state_copy(c, i):
        dr, dc = i // across, i % across
        if c % 2 == 0:
            target, holder = (dr * across, dc) if dr else (dc, 0)
        else:
            target, holder = (dc, dr * across) if dc else (dr * across, 0)
        chunk = state.at[source(holder), c]
        return remote(chunk, chunk, st_send.at[c, i], st_recv.at[c, i], "dp", peer(target))

    straight = [i for i in range(1, n) if i < across or i % across == 0]
    relayed = [i for i in range(1, n) if i not in straight]

    def feeds(c):
        return [i for i in straight if (i < across if c % 2 == 0 else i % across == 0)]

    def relay(c):
        for i in feeds(c):
            state_copy(c, i).wait_recv()
        for i in relayed:
            state_copy(c, i).start()

    def out_copy(c, i):
        src, dst = ostage.at[c, i], orecv.at[me, c]
        if i == 0:
            return pltpu.make_async_copy(src, dst, oself_sem.at[c])
        return remote(src, dst, o_send.at[c, i], o_recv.at[c, i], "dp", peer(i))

    def lines(j):
        return pl.ds(pl.multiple_of(j * width, 128), width)

    def batches(count, limit, act):
        size = next(b for b in range(min(limit, count), 0, -1) if count % b == 0)

        def step(t, carry):
            act([t * size + u for u in range(size)])
            return carry

        if count == size:
            act(list(range(size)))
        else:
            lax.fori_loop(0, count // size, step, 0)

    keep = lax.broadcasted_iota(jnp.int32, (width + EXTRA, prows), 1) + me * prows < plen[0]

    def partial_states(c, mine):
        one_size, two_size = sizes(c)
        if one_size == 1 and not mine:
            return

        def act(places):
            spots = []
            for p in places:
                one = 0 if mine else p // (per * two_size) + 1
                two, j = p // per % two_size, p % per
                h = c * span + peer(offset(c, one, two)) * per + j
                spots.append((one, two, j, h))
            keys = features(
                [pks[:, lines(h)] for *_, h in spots], [fks[h] for *_, h in spots]
            )
            values = [
                jnp.concatenate([pvs[:, lines(h)].T, jnp.ones((EXTRA, prows), BF16)], axis=0)
                for *_, h in spots
            ]
            values = [jnp.where(keep, v.astype(F32), 0.0).astype(BF16) for v in values]
            found = [dot(v, k, NT) for v, k in zip(values, keys)]
            for (one, two, j, h), f in zip(spots, found):
                part[c, one, two, lines(j), :] = f[:width].astype(BF16)
                ptot32[pl.ds(h, 1), :] = f[width : width + 1]

        batches(two_size * per * (1 if mine else one_size - 1), 4, act)

    def start_first(c):
        for i in range(1, sizes(c)[0]):
            first_copy(c, i).start()

    def pass_on(c):
        one_size, two_size = sizes(c)
        for i in range(1, one_size):
            first_copy(c, i).wait_recv()
        for two in range(1, two_size):

            def step(j, carry, two=two):
                total = part[c, 0, two, lines(j), :].astype(F32)
                for i in range(1, one_size):
                    total = total + first_in[c, i - 1, two, lines(j), :].astype(F32)
                passing[c, two - 1, lines(j), :] = total.astype(BF16)
                return carry

            lax.fori_loop(0, per, step, 0)
            second_copy(c, two).start()

    def settle(c):
        one_size, two_size = sizes(c)
        for i in range(1, two_size):
            second_copy(c, i).wait_recv()

        def step(j, carry):
            total = part[c, 0, 0, lines(j), :].astype(F32)
            for i in range(1, one_size):
                total = total + first_in[c, i - 1, 0, lines(j), :].astype(F32)
            for i in range(1, two_size):
                total = total + second_in[c, i - 1, lines(j), :].astype(F32)
            state[me, c, lines(j), :] = total.astype(BF16)
            return carry

        lax.fori_loop(0, per, step, 0)
        for i in straight:
            state_copy(c, i).start()

    causal = lax.broadcasted_iota(jnp.int32, (rows, rows), 0) <= lax.broadcasted_iota(
        jnp.int32, (rows, rows), 1
    )

    def intra(begin, end):
        def act(places):
            heads_here = [begin + p for p in places]
            cols = [lines(h) for h in heads_here]
            qf = features([qs[:, i] for i in cols], [fqs[h] for h in heads_here])
            for h, q in zip(heads_here, qf):
                phq[h] = q
            kf = [k.T for k in features([ks[:, i] for i in cols], [fks[h] for h in heads_here])]
            values = [
                jnp.concatenate([vs[:, i].T, jnp.ones((EXTRA, rows), BF16)], axis=0) for i in cols
            ]
            scores = [dot(k, q) for k, q in zip(kf, qf)]
            weights = [jnp.where(causal, x, 0.0).astype(BF16) for x in scores]
            found = [dot(v, w) for v, w in zip(values, weights)]
            for h, f in zip(heads_here, found):
                inum[h] = f

        if end > begin:
            batches(end - begin, 4, act)

    def rewards_and_tables():
        for i in range(1, n):
            for copy in info_copies(i):
                copy.wait_recv()
        total_reward = trew[0]
        for d in range(1, n):
            total_reward = total_reward + trew[d]
        mean = total_reward / n
        squares = jnp.zeros((8, 128), F32)
        for d in range(n):
            squares = squares + (trew[d] - mean) * (trew[d] - mean)
        gsum[grp] = squares
        pltpu.make_async_copy(tinfo, tsm, sm_sem).start()
        return mean

    def spread_copy(i):
        return remote(spread_all, spread_all, s_send.at[i], s_recv, "dp", peer(i))

    def squares_out():
        @pl.when(me == 0)
        def _():
            pl.semaphore_wait(barrier, groups - 1)
            for i in range(1, groups):
                group_copy(i).start()

    def squares_in():
        @pl.when(me == 0)
        def _():
            for i in range(1, groups):
                group_copy(i).wait_recv()
            spread = gsum[0]
            for g in range(1, groups):
                spread = spread + gsum[g]
            spread_all[...] = spread
            for i in range(1, n):
                spread_copy(i).start()

    live = lax.broadcasted_iota(jnp.int32, (1, rows), 1) < rlen[0, 0]

    def combine(c, piece_of):
        for step in range(1, n):
            if step not in feeds(c):
                state_copy(c, step).wait_recv()

        def act(places):
            spots = []
            for p in places:
                owner, j = p // per, p % per
                spots.append((p, owner, j, c * span + p))
            totals = [
                jnp.broadcast_to(ptot32[pl.ds(h, 1), :], (EXTRA, 2 * feat)).astype(BF16)
                for *_, h in spots
            ]
            prompts = [
                dot(jnp.concatenate([state[owner, c, lines(j), :], total], axis=0), phq[h])
                for (_, owner, j, h), total in zip(spots, totals)
            ]
            both = [x.astype(BF16).astype(F32) + inum[h] for (*_, h), x in zip(spots, prompts)]
            scales = [jnp.where(live, 1.0 / b[width : width + 1], 0.0) for b in both]
            results = [(b[:width] * r).astype(BF16).T for b, r in zip(both, scales)]
            for (p, *_), result in zip(spots, results):
                for i in range(n):
                    block = result[:BLK]
                    for q in range(1, pieces):
                        block = jnp.where(
                            piece_of[i] == q, result[q * BLK : (q + 1) * BLK], block
                        )
                    ostage[c, i, :, lines(p)] = block

        batches(n * per, 8, act)
        for i in [*range(1, n), 0]:
            out_copy(c, i).start()

    def entered():
        @pl.when(me == 0)
        def _():
            pl.semaphore_wait(entry_sem, n - 1)

    for begin in range(0, chunks, 2):
        here = range(begin, min(begin + 2, chunks))
        for c in here:
            for copy in prompt_loads(c):
                copy.wait()
            if c + 2 < chunks:
                for copy in prompt_loads(c + 2):
                    copy.start()
            partial_states(c, False)
            if c == 0:
                entered()
            start_first(c)
        for c in here:
            for copy in resp_loads(c):
                copy.start()
        for c in here:
            partial_states(c, True)
        if begin == 0:
            for i in range(1, n):
                for copy in info_copies(i):
                    copy.start()
    ptot[me] = ptot32[...].astype(BF16)
    for i in range(1, n):
        total_copy(i).start()
    for c in range(chunks):
        for copy in resp_loads(c):
            copy.wait()

    def share(part_of):
        return heads * part_of // 32 // 2 * 2

    half = -(-chunks // 2)
    intra(0, share(8))
    for c in range(half):
        pass_on(c)
    intra(share(8), share(16))
    for c in range(half, chunks):
        pass_on(c)
    mean = rewards_and_tables()
    for c in range(half):
        settle(c)
    intra(share(16), share(24))
    for c in range(half, chunks):
        settle(c)
    for c in range(half):
        relay(c)
    intra(share(24), heads)
    squares_out()
    for c in range(half, chunks):
        relay(c)
    pltpu.make_async_copy(tinfo, tsm, sm_sem).wait()
    for i in range(1, n):
        total_copy(i).wait_recv()
    totals = ptot[0].astype(F32)
    for d in range(1, n):
        totals = totals + ptot[d].astype(F32)
    ptot32[...] = totals
    piece_of = []
    for i in range(n):
        found = jnp.int32(0)
        for j in range(slot_count):
            ident = tsm[peer(i), 0, j] - me * pieces
            found = jnp.where((ident >= 0) & (ident < pieces), ident, found)
        piece_of.append(found)
    for c in range(chunks):
        combine(c, piece_of)
    squares_in()

    @pl.when(me != 0)
    def _():
        spread_copy(1).wait_recv()

    scale = jnp.sqrt(spread_all[...] / (groups * n) + 1e-06)
    adv = jnp.zeros((8, 128), F32)
    for j in range(slot_count):
        ident = slots_sm[0, j]
        src = lax.div(ident, pieces)
        start = lax.rem(ident, pieces) * BLK
        reward = jnp.zeros((8, 128), F32)
        size = jnp.int32(0)
        for d in range(n):
            reward = jnp.where(src == d, trew[d], reward)
            size = jnp.where(src == d, tsm[d, 0, slot_count], size)
        value = jnp.where(start + lane - j * BLK < size, (reward - mean) / scale, 0.0)
        adv = jnp.where((lane >= j * BLK) & (lane < (j + 1) * BLK), value, adv)
    adv_ref[...] = adv[:1]

    for i in range(1, n):
        for copy in info_copies(i):
            copy.wait_send()
        total_copy(i).wait_send()
    for c in range(chunks):
        for i in range(1, sizes(c)[0]):
            first_copy(c, i).wait_send()
        for i in range(1, sizes(c)[1]):
            second_copy(c, i).wait_send()
        for i in range(1, n):
            state_copy(c, i).wait_send()

    @pl.when(me == 0)
    def _():
        for i in range(1, groups):
            group_copy(i).wait_send()
        for i in range(1, n):
            spread_copy(i).wait_send()

    for c in range(chunks):
        for i in range(n):
            out_copy(c, i).wait()


def pick_near(pieces, slots, blocks, adv, out, adv_out, out_sem, adv_sem):
    chunks, span = blocks.shape[1], blocks.shape[3]
    copies = [pltpu.make_async_copy(adv, adv_out, adv_sem)]
    for j in range(slots.shape[1]):
        owner = lax.div(slots[0, j], pieces)
        for c in range(chunks):
            copies.append(
                pltpu.make_async_copy(
                    blocks.at[owner, c],
                    out.at[0, pl.ds(j * BLK, BLK), pl.ds(c * span, span)],
                    out_sem.at[j, c],
                )
            )
    for copy in copies:
        copy.start()
    for copy in copies:
        copy.wait()


def pick_far(slots, block_ref, adv_ref, out_ref, adv_out_ref):
    chunks, span = block_ref.shape[1], block_ref.shape[3]
    for c in range(chunks):
        out_ref[0, :, c * span : (c + 1) * span] = block_ref[0, c]
    adv_out_ref[...] = adv_ref[...]


def body(
    resp_q, resp_k, resp_v, prompt_k, prompt_v, prompt_len, resp_len, assign, rewards,
    feat_q, feat_k,
):
    n = lax.axis_size("dp")
    groups = lax.axis_size("group")
    heads, width, feat = feat_q.shape
    rows = resp_q.shape[1]
    prows = prompt_k.shape[1]
    model = resp_q.shape[2]
    own = heads // n
    chunks = next(c for c in (4, 2, 1) if own % c == 0)
    per = own // chunks
    slot_count = assign.shape[1]
    hbm = pl.BlockSpec(memory_space=pltpu.HBM)
    vmem = pl.BlockSpec(memory_space=pltpu.VMEM)
    dma = pltpu.SemaphoreType.DMA
    across = max(b for b in range(1, n + 1) if n % b == 0 and b * b <= n)
    most = max(across, n // across)
    others = max(most - 1, 1)
    entry = (per * width, 2 * feat)
    near = 2 * n * BLK * model <= 2 * 1024 * 1024
    place = pltpu.VMEM if near else jax.ShapeDtypeStruct
    arrived, adv = pl.pallas_call(
        functools.partial(kernel, n, across, groups, heads, chunks),
        out_shape=(
            place((n, chunks, BLK, model // chunks), BF16),
            place((1, slot_count * BLK), F32),
        ),
        in_specs=[hbm] * 11,
        out_specs=(pl.BlockSpec(memory_space=pl.ANY), vmem),
        scratch_shapes=[
            pltpu.VMEM((rows, model), BF16),
            pltpu.VMEM((rows, model), BF16),
            pltpu.VMEM((rows, model), BF16),
            pltpu.VMEM((heads, width, feat), BF16),
            pltpu.VMEM((heads, width, feat), BF16),
            pltpu.VMEM((prows, model), BF16),
            pltpu.VMEM((prows, model), BF16),
            pltpu.VMEM((chunks, most, most, *entry), BF16),
            pltpu.VMEM((chunks, others, most, *entry), BF16),
            pltpu.VMEM((chunks, others, *entry), BF16),
            pltpu.VMEM((chunks, others, *entry), BF16),
            pltpu.VMEM((n, chunks, *entry), BF16),
            pltpu.VMEM((heads, 2 * feat), F32),
            pltpu.VMEM((n, heads, 2 * feat), BF16),
            pltpu.VMEM((heads, 2 * feat, rows), BF16),
            pltpu.VMEM((heads, width + EXTRA, rows), F32),
            pltpu.VMEM((chunks, n, BLK, model // chunks), BF16),
            pltpu.SMEM(prompt_len.shape, jnp.int32),
            pltpu.SMEM(resp_len.shape, jnp.int32),
            pltpu.SMEM(assign.shape, jnp.int32),
            pltpu.SMEM(rewards.shape, F32),
            pltpu.VMEM((n, 8, 128), jnp.int32),
            pltpu.VMEM((n, 8, 128), F32),
            pltpu.SMEM((n, 8, 128), jnp.int32),
            pltpu.VMEM((groups, 8, 128), F32),
            pltpu.VMEM((8, 128), F32),
            dma((chunks, 7)),
            dma((chunks,)),
            dma((chunks, most)),
            dma((chunks, most)),
            dma((chunks, most)),
            dma((chunks, most)),
            dma((n,)),
            dma((n,)),
            dma((chunks, n)),
            dma((chunks, n)),
            dma((chunks, n)),
            dma((chunks, n)),
            dma((2, n)),
            dma((2, n)),
            dma((groups,)),
            dma((groups,)),
            dma((n,)),
            dma,
            dma,
            dma((4,)),
            pltpu.SemaphoreType.REGULAR,
        ],
        compiler_params=pltpu.CompilerParams(
            collective_id=0, has_side_effects=True,
            vmem_limit_bytes=(56 if near else 62) * 1024 * 1024,
        ),
        name="hedgehog",
    )(
        prompt_len, resp_len, assign, rewards, resp_q, resp_k, resp_v, prompt_k, prompt_v,
        feat_q, feat_k,
    )

    results = (
        jax.ShapeDtypeStruct((1, slot_count * BLK, model), BF16),
        jax.ShapeDtypeStruct(adv.shape, F32),
    )
    pieces = rows // BLK
    if near:
        return pl.pallas_call(
            functools.partial(pick_near, pieces),
            out_shape=results,
            in_specs=[pl.BlockSpec(memory_space=pltpu.SMEM), vmem, vmem],
            out_specs=(hbm, hbm),
            scratch_shapes=[dma((slot_count, chunks)), dma],
            name="pick",
        )(assign, *(pltpu.with_memory_space_constraint(x, pltpu.VMEM) for x in (arrived, adv)))
    return pl.pallas_call(
        pick_far,
        out_shape=results,
        grid_spec=pltpu.PrefetchScalarGridSpec(
            num_scalar_prefetch=1,
            grid=(slot_count,),
            in_specs=[
                pl.BlockSpec(
                    (1, chunks, BLK, model // chunks),
                    lambda j, slots: (lax.div(slots[0, j], pieces), 0, 0, 0),
                ),
                pl.BlockSpec(adv.shape, lambda j, slots: (0, 0)),
            ],
            out_specs=(
                pl.BlockSpec((1, BLK, model), lambda j, slots: (0, j, 0)),
                pl.BlockSpec(adv.shape, lambda j, slots: (0, 0)),
            ),
        ),
        name="pick",
    )(assign, arrived, adv)


def solution(mesh):
    return jax.shard_map(
        body,
        mesh=mesh,
        in_specs=(
            P("group", "dp", None),
            P("group", "dp", None),
            P("group", "dp", None),
            P("group", "dp", None),
            P("group", "dp", None),
            P("group"),
            P("group", "dp"),
            P("group", "dp"),
            P("group", "dp"),
            P(),
            P(),
        ),
        out_specs=(P("group", "dp", None), P("group", "dp")),
        check_vma=False,
    )
```

```python
import functools

import jax
import jax.numpy as jnp
from jax import lax
from jax.experimental import pallas as pl
from jax.experimental.pallas import tpu as pltpu
from jax.sharding import PartitionSpec as P

BLK = 64
MESH = pl.DeviceIdType.MESH
NT = (((1,), (1,)), ((), ()))
NN = (((1,), (0,)), ((), ()))
F32 = jnp.float32
BF16 = jnp.bfloat16
LOG2E = 1.4426950408889634
EXTRA = 16


def dot(a, b, dims=NN):
    return lax.dot_general(a, b, dims, preferred_element_type=F32)


def features(rows, weights):
    logits = [dot(w.T, x, NT) for x, w in zip(rows, weights)]
    tops = [jnp.max(u, axis=0, keepdims=True) for u in logits]
    lows = [jnp.min(u, axis=0, keepdims=True) for u in logits]
    ups = [jnp.exp2((u - top) * LOG2E) for u, top in zip(logits, tops)]
    downs = [jnp.exp2((low - u) * LOG2E) for u, low in zip(logits, lows)]
    up_scales = [1.0 / jnp.sum(e, axis=0, keepdims=True) for e in ups]
    down_scales = [1.0 / jnp.sum(e, axis=0, keepdims=True) for e in downs]
    return [
        jnp.concatenate([(a * r).astype(BF16), (b * q).astype(BF16)], axis=0)
        for a, b, r, q in zip(ups, downs, up_scales, down_scales)
    ]


def kernel(
    n, across, groups, heads, chunks,
    plen_hbm, rlen_hbm, slots_hbm, rew_hbm, q_hbm, k_hbm, v_hbm, pk_hbm, pv_hbm, fq_hbm, fk_hbm,
    out_ref, adv_ref,
    orecv, qs, ks, vs, fqs, fks, pks, pvs, part, first_in, passing, second_in, state,
    ptot32, ptot, row_tot, phq, inum, ostage,
    plen, rlen, slots_sm, rew_sm, tinfo, trew, tsm, gsum, spread_all,
    load_sem, oself_sem, a_send, a_recv, b_send, b_recv, t_send, t_recv,
    st_send, st_recv, o_send, o_recv,
    i_send, i_recv, g_send, g_recv, s_send, s_recv, sm_sem, small_sem, entry_sem,
):
    me = lax.axis_index("dp")
    grp = lax.axis_index("group")
    rows = qs.shape[0]
    width = fqs.shape[1]
    feat = fqs.shape[2]
    pieces = rows // BLK
    slot_count = slots_hbm.shape[1]
    own = heads // n
    per = own // chunks
    prows = pks.shape[0]

    down = n // across
    row = me // across
    col = me % across

    def peer(i):
        return (row + i // across) % down * across + (col + i % across) % across

    def source(i):
        return (row + down - i // across) % down * across + (col + across - i % across) % across

    span = n * per

    def loads(c, pairs):
        cols = pl.ds(c * span * width, span * width)
        at = pl.ds(c * span, span)
        result = []
        for hbm, buf in pairs:
            if len(buf.shape) == 3:
                src, dst = hbm.at[at], buf.at[at]
            else:
                src, dst = hbm.at[0, :, cols], buf.at[:, cols]
            result.append((src, dst))
        return result

    def prompt_loads(c):
        ends = loads(c, [(fk_hbm, fks), (pk_hbm, pks), (pv_hbm, pvs)])
        return [
            pltpu.make_async_copy(src, dst, load_sem.at[c, i]) for i, (src, dst) in enumerate(ends)
        ]

    def resp_loads(c):
        ends = loads(c, [(fq_hbm, fqs), (q_hbm, qs), (k_hbm, ks), (v_hbm, vs)])
        return [
            pltpu.make_async_copy(src, dst, load_sem.at[c, 3 + i])
            for i, (src, dst) in enumerate(ends)
        ]

    small = [
        pltpu.make_async_copy(src, dst, small_sem.at[i])
        for i, (src, dst) in enumerate(
            [(plen_hbm, plen), (rlen_hbm, rlen), (slots_hbm, slots_sm), (rew_hbm, rew_sm)]
        )
    ]
    for copy in small + [copy for c in range(min(3, chunks)) for copy in prompt_loads(c)]:
        copy.start()

    barrier = pltpu.get_barrier_semaphore()
    for i in range(1, n):

        @pl.when(peer(i) != 0)
        def _(i=i):
            pl.semaphore_signal(barrier, inc=1, device_id={"dp": peer(i)}, device_id_type=MESH)

    @pl.when(me == 0)
    def _():
        for i in range(1, groups):
            pl.semaphore_signal(
                barrier, inc=1, device_id={"group": lax.rem(grp + i, groups)}, device_id_type=MESH
            )

    @pl.when(me != 0)
    def _():
        pl.semaphore_wait(barrier, n - 1)
        pl.semaphore_signal(entry_sem, inc=1, device_id={"dp": 0}, device_id_type=MESH)

    for copy in small:
        copy.wait()
    lane = lax.broadcasted_iota(jnp.int32, (8, 128), 1)
    info = jnp.where(lane == slot_count, rlen[0, 0], 0)
    for j in range(slot_count):
        info = jnp.where(lane == j, slots_sm[0, j], info)
    tinfo[me] = info
    trew[me] = jnp.full((8, 128), rew_sm[0, 0], F32)

    def remote(src, dst, send, recv, axis, target):
        return pltpu.make_async_remote_copy(
            src_ref=src, dst_ref=dst, send_sem=send, recv_sem=recv,
            device_id={axis: target}, device_id_type=MESH,
        )

    def info_copies(i):
        return [
            remote(tinfo.at[me], tinfo.at[me], i_send.at[0, i], i_recv.at[0, i], "dp", peer(i)),
            remote(trew.at[me], trew.at[me], i_send.at[1, i], i_recv.at[1, i], "dp", peer(i)),
        ]

    def group_copy(i):
        return remote(
            gsum.at[grp], gsum.at[grp], g_send.at[i], g_recv.at[i], "group",
            lax.rem(grp + i, groups),
        )

    def total_copy(i):
        here = row_tot.at[row] if i % across == 0 else ptot.at[col]
        return remote(here, here, t_send.at[i], t_recv.at[i], "dp", peer(i))

    def start_totals():
        ptot[col] = ptot32[...].astype(BF16)
        for i in range(1, across):
            total_copy(i).start()

    def add_up(rows_of):
        total = rows_of[0].astype(F32)
        for d in range(1, rows_of.shape[0]):
            total = total + rows_of[d].astype(F32)
        return total

    def pass_totals():
        for i in range(1, across):
            total_copy(i).wait_recv()
        row_tot[row] = add_up(ptot).astype(BF16)
        for i in range(across, n, across):
            total_copy(i).start()

    def settle_totals():
        for i in range(across, n, across):
            total_copy(i).wait_recv()
        ptot32[...] = add_up(row_tot)

    def sizes(c):
        return (across, down) if c % 2 == 0 else (down, across)

    def offset(c, one, two):
        return two * across + one if c % 2 == 0 else one * across + two

    def first_copy(c, i):
        span = pl.ds(0, sizes(c)[1])
        return remote(
            part.at[c, i, span], first_in.at[c, i - 1, span], a_send.at[c, i], a_recv.at[c, i],
            "dp", peer(offset(c, i, 0)),
        )

    def second_copy(c, i):
        return remote(
            passing.at[c, i - 1], second_in.at[c, i - 1], b_send.at[c, i], b_recv.at[c, i],
            "dp", peer(offset(c, 0, i)),
        )

    def state_copy(c, i):
        dr, dc = i // across, i % across
        if c % 2 == 0:
            target, holder = (dr * across, dc) if dr else (dc, 0)
        else:
            target, holder = (dc, dr * across) if dc else (dr * across, 0)
        chunk = state.at[source(holder), c]
        return remote(chunk, chunk, st_send.at[c, i], st_recv.at[c, i], "dp", peer(target))

    straight = [i for i in range(1, n) if i < across or i % across == 0]
    relayed = [i for i in range(1, n) if i not in straight]

    def feeds(c):
        return [i for i in straight if (i < across if c % 2 == 0 else i % across == 0)]

    def relay(c):
        for i in feeds(c):
            state_copy(c, i).wait_recv()
        for i in relayed:
            state_copy(c, i).start()

    def out_copy(c, i):
        src, dst = ostage.at[c, i], orecv.at[me, c]
        if i == 0:
            return pltpu.make_async_copy(src, dst, oself_sem.at[c])
        return remote(src, dst, o_send.at[c, i], o_recv.at[c, i], "dp", peer(i))

    def lines(j):
        return pl.ds(pl.multiple_of(j * width, 128), width)

    def batches(count, limit, act):
        size = next(b for b in range(min(limit, count), 0, -1) if count % b == 0)

        def step(t, carry):
            act([t * size + u for u in range(size)])
            return carry

        if count == size:
            act(list(range(size)))
        else:
            lax.fori_loop(0, count // size, step, 0)

    keep = lax.broadcasted_iota(jnp.int32, (width + EXTRA, prows), 1) + me * prows < plen[0]

    def partial_states(c, mine):
        one_size, two_size = sizes(c)
        if one_size == 1 and not mine:
            return

        def act(places):
            spots = []
            for p in places:
                one = 0 if mine else p // (per * two_size) + 1
                two, j = p // per % two_size, p % per
                h = c * span + peer(offset(c, one, two)) * per + j
                spots.append((one, two, j, h))
            keys = features(
                [pks[:, lines(h)] for *_, h in spots], [fks[h] for *_, h in spots]
            )
            values = [
                jnp.concatenate([pvs[:, lines(h)].T, jnp.ones((EXTRA, prows), BF16)], axis=0)
                for *_, h in spots
            ]
            values = [jnp.where(keep, v.astype(F32), 0.0).astype(BF16) for v in values]
            found = [dot(v, k, NT) for v, k in zip(values, keys)]
            for (one, two, j, h), f in zip(spots, found):
                part[c, one, two, lines(j), :] = f[:width].astype(BF16)
                ptot32[pl.ds(h, 1), :] = f[width : width + 1]

        batches(two_size * per * (1 if mine else one_size - 1), 4, act)

    def start_first(c):
        for i in range(1, sizes(c)[0]):
            first_copy(c, i).start()

    def pass_on(c):
        one_size, two_size = sizes(c)
        for i in range(1, one_size):
            first_copy(c, i).wait_recv()
        for two in range(1, two_size):

            def step(j, carry, two=two):
                total = part[c, 0, two, lines(j), :].astype(F32)
                for i in range(1, one_size):
                    total = total + first_in[c, i - 1, two, lines(j), :].astype(F32)
                passing[c, two - 1, lines(j), :] = total.astype(BF16)
                return carry

            lax.fori_loop(0, per, step, 0)
            second_copy(c, two).start()

    def settle(c):
        one_size, two_size = sizes(c)
        for i in range(1, two_size):
            second_copy(c, i).wait_recv()

        def step(j, carry):
            total = part[c, 0, 0, lines(j), :].astype(F32)
            for i in range(1, one_size):
                total = total + first_in[c, i - 1, 0, lines(j), :].astype(F32)
            for i in range(1, two_size):
                total = total + second_in[c, i - 1, lines(j), :].astype(F32)
            state[me, c, lines(j), :] = total.astype(BF16)
            return carry

        lax.fori_loop(0, per, step, 0)
        for i in straight:
            state_copy(c, i).start()

    causal = lax.broadcasted_iota(jnp.int32, (rows, rows), 0) <= lax.broadcasted_iota(
        jnp.int32, (rows, rows), 1
    )

    def intra(begin, end):
        def act(places):
            heads_here = [begin + p for p in places]
            cols = [lines(h) for h in heads_here]
            qf = features([qs[:, i] for i in cols], [fqs[h] for h in heads_here])
            for h, q in zip(heads_here, qf):
                phq[h] = q
            kf = [k.T for k in features([ks[:, i] for i in cols], [fks[h] for h in heads_here])]
            values = [
                jnp.concatenate([vs[:, i].T, jnp.ones((EXTRA, rows), BF16)], axis=0) for i in cols
            ]
            scores = [dot(k, q) for k, q in zip(kf, qf)]
            weights = [jnp.where(causal, x, 0.0).astype(BF16) for x in scores]
            found = [dot(v, w) for v, w in zip(values, weights)]
            for h, f in zip(heads_here, found):
                inum[h] = f

        if end > begin:
            batches(end - begin, 4, act)

    def rewards_and_tables():
        for i in range(1, n):
            for copy in info_copies(i):
                copy.wait_recv()
        total_reward = trew[0]
        for d in range(1, n):
            total_reward = total_reward + trew[d]
        mean = total_reward / n
        squares = jnp.zeros((8, 128), F32)
        for d in range(n):
            squares = squares + (trew[d] - mean) * (trew[d] - mean)
        gsum[grp] = squares
        pltpu.make_async_copy(tinfo, tsm, sm_sem).start()
        return mean

    def spread_copy(i):
        return remote(spread_all, spread_all, s_send.at[i], s_recv, "dp", peer(i))

    def squares_out():
        @pl.when(me == 0)
        def _():
            pl.semaphore_wait(barrier, groups - 1)
            for i in range(1, groups):
                group_copy(i).start()

    def squares_in():
        @pl.when(me == 0)
        def _():
            for i in range(1, groups):
                group_copy(i).wait_recv()
            spread = gsum[0]
            for g in range(1, groups):
                spread = spread + gsum[g]
            spread_all[...] = spread
            for i in range(1, n):
                spread_copy(i).start()

    live = lax.broadcasted_iota(jnp.int32, (1, rows), 1) < rlen[0, 0]

    def combine(c, piece_of):
        for step in range(1, n):
            if step not in feeds(c):
                state_copy(c, step).wait_recv()

        def act(places):
            spots = []
            for p in places:
                owner, j = p // per, p % per
                spots.append((p, owner, j, c * span + p))
            totals = [
                jnp.broadcast_to(ptot32[pl.ds(h, 1), :], (EXTRA, 2 * feat)).astype(BF16)
                for *_, h in spots
            ]
            prompts = [
                dot(jnp.concatenate([state[owner, c, lines(j), :], total], axis=0), phq[h])
                for (_, owner, j, h), total in zip(spots, totals)
            ]
            both = [x.astype(BF16).astype(F32) + inum[h] for (*_, h), x in zip(spots, prompts)]
            scales = [jnp.where(live, 1.0 / b[width : width + 1], 0.0) for b in both]
            results = [(b[:width] * r).astype(BF16).T for b, r in zip(both, scales)]
            for (p, *_), result in zip(spots, results):
                for i in range(n):
                    block = result[:BLK]
                    for q in range(1, pieces):
                        block = jnp.where(
                            piece_of[i] == q, result[q * BLK : (q + 1) * BLK], block
                        )
                    ostage[c, i, :, lines(p)] = block

        batches(n * per, 8, act)
        for i in [*range(1, n), 0]:
            out_copy(c, i).start()

    def entered():
        @pl.when(me == 0)
        def _():
            pl.semaphore_wait(entry_sem, n - 1)

    for begin in range(0, chunks, 2):
        here = range(begin, min(begin + 2, chunks))
        for c in here:
            for copy in prompt_loads(c):
                copy.wait()
            if c + 3 < chunks:
                for copy in prompt_loads(c + 3):
                    copy.start()
            partial_states(c, False)
            if c == 0:
                entered()
            start_first(c)
        for c in here:
            for copy in resp_loads(c):
                copy.start()
        if begin == 0:
            for i in range(1, n):
                for copy in info_copies(i):
                    copy.start()
    for c in range(chunks):
        partial_states(c, True)
    start_totals()
    for c in range(chunks):
        for copy in resp_loads(c):
            copy.wait()

    def share(part_of):
        return heads * part_of // 32 // 2 * 2

    half = -(-chunks // 2)
    intra(0, share(8))
    for c in range(half):
        pass_on(c)
    intra(share(8), share(16))
    for c in range(half, chunks):
        pass_on(c)
    pass_totals()
    mean = rewards_and_tables()
    for c in range(half):
        settle(c)
    intra(share(16), share(24))
    for c in range(half, chunks):
        settle(c)
    for c in range(half):
        relay(c)
    intra(share(24), heads)
    squares_out()
    for c in range(half, chunks):
        relay(c)
    pltpu.make_async_copy(tinfo, tsm, sm_sem).wait()
    settle_totals()
    piece_of = []
    for i in range(n):
        found = jnp.int32(0)
        for j in range(slot_count):
            ident = tsm[peer(i), 0, j] - me * pieces
            found = jnp.where((ident >= 0) & (ident < pieces), ident, found)
        piece_of.append(found)
    for c in range(chunks):
        combine(c, piece_of)
    squares_in()

    @pl.when(me != 0)
    def _():
        spread_copy(1).wait_recv()

    scale = jnp.sqrt(spread_all[...] / (groups * n) + 1e-06)
    adv = jnp.zeros((8, 128), F32)
    for j in range(slot_count):
        ident = slots_sm[0, j]
        src = lax.div(ident, pieces)
        start = lax.rem(ident, pieces) * BLK
        reward = jnp.zeros((8, 128), F32)
        size = jnp.int32(0)
        for d in range(n):
            reward = jnp.where(src == d, trew[d], reward)
            size = jnp.where(src == d, tsm[d, 0, slot_count], size)
        value = jnp.where(start + lane - j * BLK < size, (reward - mean) / scale, 0.0)
        adv = jnp.where((lane >= j * BLK) & (lane < (j + 1) * BLK), value, adv)
    adv_ref[...] = adv[:1]

    for i in range(1, n):
        for copy in info_copies(i):
            copy.wait_send()
        if i < across or i % across == 0:
            total_copy(i).wait_send()
    for c in range(chunks):
        for i in range(1, sizes(c)[0]):
            first_copy(c, i).wait_send()
        for i in range(1, sizes(c)[1]):
            second_copy(c, i).wait_send()
        for i in range(1, n):
            state_copy(c, i).wait_send()

    @pl.when(me == 0)
    def _():
        for i in range(1, groups):
            group_copy(i).wait_send()
        for i in range(1, n):
            spread_copy(i).wait_send()

    for c in range(chunks):
        for i in range(n):
            out_copy(c, i).wait()
        for j in range(slot_count):
            src = lax.div(slots_sm[0, j], pieces)
            block = orecv[0, c]
            for d in range(1, n):
                block = jnp.where(src == d, orecv[d, c], block)
            out_ref[0, j * BLK : (j + 1) * BLK, c * span * width : (c + 1) * span * width] = block


def body(
    resp_q, resp_k, resp_v, prompt_k, prompt_v, prompt_len, resp_len, assign, rewards,
    feat_q, feat_k,
):
    n = lax.axis_size("dp")
    groups = lax.axis_size("group")
    heads, width, feat = feat_q.shape
    rows = resp_q.shape[1]
    prows = prompt_k.shape[1]
    model = resp_q.shape[2]
    own = heads // n
    chunks = next(c for c in (4, 2, 1) if own % c == 0)
    per = own // chunks
    slot_count = assign.shape[1]
    hbm = pl.BlockSpec(memory_space=pltpu.HBM)
    vmem = pl.BlockSpec(memory_space=pltpu.VMEM)
    dma = pltpu.SemaphoreType.DMA
    across = max(b for b in range(1, n + 1) if n % b == 0 and b * b <= n)
    most = max(across, n // across)
    others = max(most - 1, 1)
    entry = (per * width, 2 * feat)
    return pl.pallas_call(
        functools.partial(kernel, n, across, groups, heads, chunks),
        out_shape=(
            pltpu.VMEM((1, slot_count * BLK, model), BF16),
            pltpu.VMEM((1, slot_count * BLK), F32),
        ),
        in_specs=[hbm] * 11,
        out_specs=(vmem, vmem),
        scratch_shapes=[
            pltpu.VMEM((n, chunks, BLK, model // chunks), BF16),
            pltpu.VMEM((rows, model), BF16),
            pltpu.VMEM((rows, model), BF16),
            pltpu.VMEM((rows, model), BF16),
            pltpu.VMEM((heads, width, feat), BF16),
            pltpu.VMEM((heads, width, feat), BF16),
            pltpu.VMEM((prows, model), BF16),
            pltpu.VMEM((prows, model), BF16),
            pltpu.VMEM((chunks, most, most, *entry), BF16),
            pltpu.VMEM((chunks, others, most, *entry), BF16),
            pltpu.VMEM((chunks, others, *entry), BF16),
            pltpu.VMEM((chunks, others, *entry), BF16),
            pltpu.VMEM((n, chunks, *entry), BF16),
            pltpu.VMEM((heads, 2 * feat), F32),
            pltpu.VMEM((across, heads, 2 * feat), BF16),
            pltpu.VMEM((n // across, heads, 2 * feat), BF16),
            pltpu.VMEM((heads, 2 * feat, rows), BF16),
            pltpu.VMEM((heads, width + EXTRA, rows), F32),
            pltpu.VMEM((chunks, n, BLK, model // chunks), BF16),
            pltpu.SMEM(prompt_len.shape, jnp.int32),
            pltpu.SMEM(resp_len.shape, jnp.int32),
            pltpu.SMEM(assign.shape, jnp.int32),
            pltpu.SMEM(rewards.shape, F32),
            pltpu.VMEM((n, 8, 128), jnp.int32),
            pltpu.VMEM((n, 8, 128), F32),
            pltpu.SMEM((n, 8, 128), jnp.int32),
            pltpu.VMEM((groups, 8, 128), F32),
            pltpu.VMEM((8, 128), F32),
            dma((chunks, 7)),
            dma((chunks,)),
            dma((chunks, most)),
            dma((chunks, most)),
            dma((chunks, most)),
            dma((chunks, most)),
            dma((n,)),
            dma((n,)),
            dma((chunks, n)),
            dma((chunks, n)),
            dma((chunks, n)),
            dma((chunks, n)),
            dma((2, n)),
            dma((2, n)),
            dma((groups,)),
            dma((groups,)),
            dma((n,)),
            dma,
            dma,
            dma((4,)),
            pltpu.SemaphoreType.REGULAR,
        ],
        compiler_params=pltpu.CompilerParams(
            collective_id=0, has_side_effects=True,
            vmem_limit_bytes=56 * 1024 * 1024,
        ),
        name="hedgehog",
    )(
        prompt_len, resp_len, assign, rewards, resp_q, resp_k, resp_v, prompt_k, prompt_v,
        feat_q, feat_k,
    )


def solution(mesh):
    return jax.shard_map(
        body,
        mesh=mesh,
        in_specs=(
            P("group", "dp", None),
            P("group", "dp", None),
            P("group", "dp", None),
            P("group", "dp", None),
            P("group", "dp", None),
            P("group"),
            P("group", "dp"),
            P("group", "dp"),
            P("group", "dp"),
            P(),
            P(),
        ),
        out_specs=(P("group", "dp", None), P("group", "dp")),
        check_vma=False,
    )
```

```python
import functools

import jax
import jax.numpy as jnp
from jax import lax
from jax.experimental import pallas as pl
from jax.experimental.pallas import tpu as pltpu
from jax.sharding import PartitionSpec as P

BLK = 64
MESH = pl.DeviceIdType.MESH
NT = (((1,), (1,)), ((), ()))
NN = (((1,), (0,)), ((), ()))
F32 = jnp.float32
BF16 = jnp.bfloat16
LOG2E = 1.4426950408889634
EXTRA = 16


def dot(a, b, dims=NN):
    return lax.dot_general(a, b, dims, preferred_element_type=F32)


def features(rows, weights):
    logits = [dot(w.T, x, NT) for x, w in zip(rows, weights)]
    tops = [jnp.max(u, axis=0, keepdims=True) for u in logits]
    lows = [jnp.min(u, axis=0, keepdims=True) for u in logits]
    ups = [jnp.exp2((u - top) * LOG2E) for u, top in zip(logits, tops)]
    downs = [jnp.exp2((low - u) * LOG2E) for u, low in zip(logits, lows)]
    up_scales = [1.0 / jnp.sum(e, axis=0, keepdims=True) for e in ups]
    down_scales = [1.0 / jnp.sum(e, axis=0, keepdims=True) for e in downs]
    return [
        jnp.concatenate([(a * r).astype(BF16), (b * q).astype(BF16)], axis=0)
        for a, b, r, q in zip(ups, downs, up_scales, down_scales)
    ]


def kernel(
    n, across, groups, heads, chunks,
    plen_hbm, rlen_hbm, slots_hbm, rew_hbm, q_hbm, k_hbm, v_hbm, pk_hbm, pv_hbm, fq_hbm, fk_hbm,
    out_ref, adv_ref,
    orecv, qs, ks, vs, fqs, fks, pks, pvs, part, first_in, passing, second_in, state,
    ptot32, ptot, row_tot, phq, inum, ostage,
    plen, rlen, slots_sm, rew_sm, tinfo, trew, tsm, gsum, spread_all,
    load_sem, oself_sem, a_send, a_recv, b_send, b_recv, t_send, t_recv,
    st_send, st_recv, o_send, o_recv,
    i_send, i_recv, g_send, g_recv, s_send, s_recv, sm_sem, small_sem, entry_sem,
):
    me = lax.axis_index("dp")
    grp = lax.axis_index("group")
    rows = qs.shape[0]
    width = fqs.shape[1]
    feat = fqs.shape[2]
    pieces = rows // BLK
    slot_count = slots_hbm.shape[1]
    own = heads // n
    per = own // chunks
    prows = pks.shape[0]

    down = n // across
    row = me // across
    col = me % across

    def peer(i):
        return (row + i // across) % down * across + (col + i % across) % across

    def source(i):
        return (row + down - i // across) % down * across + (col + across - i % across) % across

    span = n * per

    def loads(c, pairs):
        cols = pl.ds(c * span * width, span * width)
        at = pl.ds(c * span, span)
        result = []
        for hbm, buf in pairs:
            if len(buf.shape) == 3:
                src, dst = hbm.at[at], buf.at[at]
            else:
                src, dst = hbm.at[0, :, cols], buf.at[:, cols]
            result.append((src, dst))
        return result

    def prompt_loads(c):
        ends = loads(c, [(fk_hbm, fks), (pk_hbm, pks), (pv_hbm, pvs)])
        return [
            pltpu.make_async_copy(src, dst, load_sem.at[c, i]) for i, (src, dst) in enumerate(ends)
        ]

    def resp_loads(c):
        ends = loads(c, [(fq_hbm, fqs), (q_hbm, qs), (k_hbm, ks), (v_hbm, vs)])
        return [
            pltpu.make_async_copy(src, dst, load_sem.at[c, 3 + i])
            for i, (src, dst) in enumerate(ends)
        ]

    small = [
        pltpu.make_async_copy(src, dst, small_sem.at[i])
        for i, (src, dst) in enumerate(
            [(plen_hbm, plen), (rlen_hbm, rlen), (slots_hbm, slots_sm), (rew_hbm, rew_sm)]
        )
    ]
    for copy in small + [copy for c in range(min(3, chunks)) for copy in prompt_loads(c)]:
        copy.start()

    barrier = pltpu.get_barrier_semaphore()
    for i in range(1, n):

        @pl.when(peer(i) != 0)
        def _(i=i):
            pl.semaphore_signal(barrier, inc=1, device_id={"dp": peer(i)}, device_id_type=MESH)

    @pl.when(me == 0)
    def _():
        for i in range(1, groups):
            pl.semaphore_signal(
                barrier, inc=1, device_id={"group": lax.rem(grp + i, groups)}, device_id_type=MESH
            )

    @pl.when(me != 0)
    def _():
        pl.semaphore_wait(barrier, n - 1)
        pl.semaphore_signal(entry_sem, inc=1, device_id={"dp": 0}, device_id_type=MESH)

    for copy in small:
        copy.wait()
    lane = lax.broadcasted_iota(jnp.int32, (8, 128), 1)
    info = jnp.where(lane == slot_count, rlen[0, 0], 0)
    for j in range(slot_count):
        info = jnp.where(lane == j, slots_sm[0, j], info)
    tinfo[me] = info
    trew[me] = jnp.full((8, 128), rew_sm[0, 0], F32)

    def remote(src, dst, send, recv, axis, target):
        return pltpu.make_async_remote_copy(
            src_ref=src, dst_ref=dst, send_sem=send, recv_sem=recv,
            device_id={axis: target}, device_id_type=MESH,
        )

    def info_copies(i):
        return [
            remote(tinfo.at[me], tinfo.at[me], i_send.at[0, i], i_recv.at[0, i], "dp", peer(i)),
            remote(trew.at[me], trew.at[me], i_send.at[1, i], i_recv.at[1, i], "dp", peer(i)),
        ]

    def group_copy(i):
        return remote(
            gsum.at[grp], gsum.at[grp], g_send.at[i], g_recv.at[i], "group",
            lax.rem(grp + i, groups),
        )

    def total_copy(i):
        here = row_tot.at[row] if i % across == 0 else ptot.at[col]
        return remote(here, here, t_send.at[i], t_recv.at[i], "dp", peer(i))

    def start_totals():
        ptot[col] = ptot32[...].astype(BF16)
        for i in range(1, across):
            total_copy(i).start()

    def add_up(rows_of):
        total = rows_of[0].astype(F32)
        for d in range(1, rows_of.shape[0]):
            total = total + rows_of[d].astype(F32)
        return total

    def pass_totals():
        for i in range(1, across):
            total_copy(i).wait_recv()
        row_tot[row] = add_up(ptot).astype(BF16)
        for i in range(across, n, across):
            total_copy(i).start()

    def settle_totals():
        for i in range(across, n, across):
            total_copy(i).wait_recv()
        ptot32[...] = add_up(row_tot)

    def sizes(c):
        return (across, down) if c % 2 == 0 else (down, across)

    def offset(c, one, two):
        return two * across + one if c % 2 == 0 else one * across + two

    def first_copy(c, i):
        span = pl.ds(0, sizes(c)[1])
        return remote(
            part.at[c, i, span], first_in.at[c, i - 1, span], a_send.at[c, i], a_recv.at[c, i],
            "dp", peer(offset(c, i, 0)),
        )

    def second_copy(c, i):
        return remote(
            passing.at[c, i - 1], second_in.at[c, i - 1], b_send.at[c, i], b_recv.at[c, i],
            "dp", peer(offset(c, 0, i)),
        )

    def state_copy(c, i):
        dr, dc = i // across, i % across
        if c % 2 == 0:
            target, holder = (dr * across, dc) if dr else (dc, 0)
        else:
            target, holder = (dc, dr * across) if dc else (dr * across, 0)
        chunk = state.at[source(holder), c]
        return remote(chunk, chunk, st_send.at[c, i], st_recv.at[c, i], "dp", peer(target))

    straight = [i for i in range(1, n) if i < across or i % across == 0]
    relayed = [i for i in range(1, n) if i not in straight]

    def feeds(c):
        return [i for i in straight if (i < across if c % 2 == 0 else i % across == 0)]

    def relay(c):
        for i in feeds(c):
            state_copy(c, i).wait_recv()
        for i in relayed:
            state_copy(c, i).start()

    def out_copy(c, i):
        src, dst = ostage.at[c, i], orecv.at[me, c]
        if i == 0:
            return pltpu.make_async_copy(src, dst, oself_sem.at[c])
        return remote(src, dst, o_send.at[c, i], o_recv.at[c, i], "dp", peer(i))

    def lines(j):
        return pl.ds(pl.multiple_of(j * width, 128), width)

    def batches(count, limit, act):
        size = next(b for b in range(min(limit, count), 0, -1) if count % b == 0)

        def step(t, carry):
            act([t * size + u for u in range(size)])
            return carry

        if count == size:
            act(list(range(size)))
        else:
            lax.fori_loop(0, count // size, step, 0)

    keep = lax.broadcasted_iota(jnp.int32, (width + EXTRA, prows), 1) + me * prows < plen[0]

    def partial_states(c, mine):
        one_size, two_size = sizes(c)
        if one_size == 1 and not mine:
            return

        def act(places):
            spots = []
            for p in places:
                one = 0 if mine else p // (per * two_size) + 1
                two, j = p // per % two_size, p % per
                h = c * span + peer(offset(c, one, two)) * per + j
                spots.append((one, two, j, h))
            keys = features(
                [pks[:, lines(h)] for *_, h in spots], [fks[h] for *_, h in spots]
            )
            values = [
                jnp.concatenate([pvs[:, lines(h)].T, jnp.ones((EXTRA, prows), BF16)], axis=0)
                for *_, h in spots
            ]
            values = [jnp.where(keep, v.astype(F32), 0.0).astype(BF16) for v in values]
            found = [dot(v, k, NT) for v, k in zip(values, keys)]
            for (one, two, j, h), f in zip(spots, found):
                part[c, one, two, lines(j), :] = f[:width].astype(BF16)
                ptot32[pl.ds(h, 1), :] = f[width : width + 1]

        batches(two_size * per * (1 if mine else one_size - 1), 4, act)

    def start_first(c):
        for i in range(1, sizes(c)[0]):
            first_copy(c, i).start()

    def pass_on(c):
        one_size, two_size = sizes(c)
        for i in range(1, one_size):
            first_copy(c, i).wait_recv()
        for two in range(1, two_size):

            def step(j, carry, two=two):
                total = part[c, 0, two, lines(j), :].astype(F32)
                for i in range(1, one_size):
                    total = total + first_in[c, i - 1, two, lines(j), :].astype(F32)
                passing[c, two - 1, lines(j), :] = total.astype(BF16)
                return carry

            lax.fori_loop(0, per, step, 0)
            second_copy(c, two).start()

    def settle(c):
        one_size, two_size = sizes(c)
        for i in range(1, two_size):
            second_copy(c, i).wait_recv()

        def step(j, carry):
            total = part[c, 0, 0, lines(j), :].astype(F32)
            for i in range(1, one_size):
                total = total + first_in[c, i - 1, 0, lines(j), :].astype(F32)
            for i in range(1, two_size):
                total = total + second_in[c, i - 1, lines(j), :].astype(F32)
            state[me, c, lines(j), :] = total.astype(BF16)
            return carry

        lax.fori_loop(0, per, step, 0)
        for i in straight:
            state_copy(c, i).start()

    causal = lax.broadcasted_iota(jnp.int32, (rows, rows), 0) <= lax.broadcasted_iota(
        jnp.int32, (rows, rows), 1
    )

    def intra(begin, end):
        def act(places):
            heads_here = [begin + p for p in places]
            cols = [lines(h) for h in heads_here]
            qf = features([qs[:, i] for i in cols], [fqs[h] for h in heads_here])
            for h, q in zip(heads_here, qf):
                phq[h] = q
            kf = [k.T for k in features([ks[:, i] for i in cols], [fks[h] for h in heads_here])]
            values = [
                jnp.concatenate([vs[:, i].T, jnp.ones((EXTRA, rows), BF16)], axis=0) for i in cols
            ]
            scores = [dot(k, q) for k, q in zip(kf, qf)]
            weights = [jnp.where(causal, x, 0.0).astype(BF16) for x in scores]
            found = [dot(v, w) for v, w in zip(values, weights)]
            for h, f in zip(heads_here, found):
                inum[h] = f

        if end > begin:
            batches(end - begin, 4, act)

    def rewards_and_tables():
        for i in range(1, n):
            for copy in info_copies(i):
                copy.wait_recv()
        total_reward = trew[0]
        for d in range(1, n):
            total_reward = total_reward + trew[d]
        mean = total_reward / n
        squares = jnp.zeros((8, 128), F32)
        for d in range(n):
            squares = squares + (trew[d] - mean) * (trew[d] - mean)
        gsum[grp] = squares
        pltpu.make_async_copy(tinfo, tsm, sm_sem).start()
        return mean

    def spread_copy(i):
        return remote(spread_all, spread_all, s_send.at[i], s_recv, "dp", peer(i))

    def squares_out():
        @pl.when(me == 0)
        def _():
            pl.semaphore_wait(barrier, groups - 1)
            for i in range(1, groups):
                group_copy(i).start()

    def squares_in():
        @pl.when(me == 0)
        def _():
            for i in range(1, groups):
                group_copy(i).wait_recv()
            spread = gsum[0]
            for g in range(1, groups):
                spread = spread + gsum[g]
            spread_all[...] = spread
            for i in range(1, n):
                spread_copy(i).start()

    live = lax.broadcasted_iota(jnp.int32, (1, rows), 1) < rlen[0, 0]

    def combine(c, piece_of):
        for step in range(1, n):
            if step not in feeds(c):
                state_copy(c, step).wait_recv()

        def act(places):
            spots = []
            for p in places:
                owner, j = p // per, p % per
                spots.append((p, owner, j, c * span + p))
            totals = [
                jnp.broadcast_to(ptot32[pl.ds(h, 1), :], (EXTRA, 2 * feat)).astype(BF16)
                for *_, h in spots
            ]
            prompts = [
                dot(jnp.concatenate([state[owner, c, lines(j), :], total], axis=0), phq[h])
                for (_, owner, j, h), total in zip(spots, totals)
            ]
            both = [x.astype(BF16).astype(F32) + inum[h] for (*_, h), x in zip(spots, prompts)]
            scales = [jnp.where(live, 1.0 / b[width : width + 1], 0.0) for b in both]
            results = [(b[:width] * r).astype(BF16).T for b, r in zip(both, scales)]
            for (p, *_), result in zip(spots, results):
                for i in range(n):
                    block = result[:BLK]
                    for q in range(1, pieces):
                        block = jnp.where(
                            piece_of[i] == q, result[q * BLK : (q + 1) * BLK], block
                        )
                    ostage[c, i, :, lines(p)] = block

        batches(n * per, 8, act)
        for i in [*relayed, *straight, 0]:
            out_copy(c, i).start()

    def entered():
        @pl.when(me == 0)
        def _():
            pl.semaphore_wait(entry_sem, n - 1)

    for begin in range(0, chunks, 2):
        here = range(begin, min(begin + 2, chunks))
        for c in here:
            for copy in prompt_loads(c):
                copy.wait()
            if c + 3 < chunks:
                for copy in prompt_loads(c + 3):
                    copy.start()
            partial_states(c, False)
            if c == 0:
                entered()
            start_first(c)
        if begin == 0:
            for i in range(1, n):
                for copy in info_copies(i):
                    copy.start()
    for c in range(chunks):
        for copy in resp_loads(c):
            copy.start()
    for c in range(chunks):
        partial_states(c, True)
    start_totals()
    for c in range(chunks):
        for copy in resp_loads(c):
            copy.wait()

    def share(part_of):
        return heads * part_of // 32 // 2 * 2

    half = -(-chunks // 2)
    intra(0, share(8))
    for c in range(half):
        pass_on(c)
    intra(share(8), share(16))
    for c in range(half, chunks):
        pass_on(c)
    pass_totals()
    mean = rewards_and_tables()
    for c in range(half):
        settle(c)
    intra(share(16), share(24))
    for c in range(half, chunks):
        settle(c)
    for c in range(half):
        relay(c)
    intra(share(24), heads)
    squares_out()
    for c in range(half, chunks):
        relay(c)
    pltpu.make_async_copy(tinfo, tsm, sm_sem).wait()
    settle_totals()
    piece_of = []
    for i in range(n):
        found = jnp.int32(0)
        for j in range(slot_count):
            ident = tsm[peer(i), 0, j] - me * pieces
            found = jnp.where((ident >= 0) & (ident < pieces), ident, found)
        piece_of.append(found)
    for c in range(chunks):
        combine(c, piece_of)
    squares_in()

    @pl.when(me != 0)
    def _():
        spread_copy(1).wait_recv()

    scale = jnp.sqrt(spread_all[...] / (groups * n) + 1e-06)
    adv = jnp.zeros((8, 128), F32)
    for j in range(slot_count):
        ident = slots_sm[0, j]
        src = lax.div(ident, pieces)
        start = lax.rem(ident, pieces) * BLK
        reward = jnp.zeros((8, 128), F32)
        size = jnp.int32(0)
        for d in range(n):
            reward = jnp.where(src == d, trew[d], reward)
            size = jnp.where(src == d, tsm[d, 0, slot_count], size)
        value = jnp.where(start + lane - j * BLK < size, (reward - mean) / scale, 0.0)
        adv = jnp.where((lane >= j * BLK) & (lane < (j + 1) * BLK), value, adv)
    adv_ref[...] = adv[:1]

    for i in range(1, n):
        for copy in info_copies(i):
            copy.wait_send()
        if i < across or i % across == 0:
            total_copy(i).wait_send()
    for c in range(chunks):
        for i in range(1, sizes(c)[0]):
            first_copy(c, i).wait_send()
        for i in range(1, sizes(c)[1]):
            second_copy(c, i).wait_send()
        for i in range(1, n):
            state_copy(c, i).wait_send()

    @pl.when(me == 0)
    def _():
        for i in range(1, groups):
            group_copy(i).wait_send()
        for i in range(1, n):
            spread_copy(i).wait_send()

    for c in range(chunks):
        for i in range(n):
            out_copy(c, i).wait()
        for j in range(slot_count):
            src = lax.div(slots_sm[0, j], pieces)
            block = orecv[0, c]
            for d in range(1, n):
                block = jnp.where(src == d, orecv[d, c], block)
            out_ref[0, j * BLK : (j + 1) * BLK, c * span * width : (c + 1) * span * width] = block


def body(
    resp_q, resp_k, resp_v, prompt_k, prompt_v, prompt_len, resp_len, assign, rewards,
    feat_q, feat_k,
):
    n = lax.axis_size("dp")
    groups = lax.axis_size("group")
    heads, width, feat = feat_q.shape
    rows = resp_q.shape[1]
    prows = prompt_k.shape[1]
    model = resp_q.shape[2]
    own = heads // n
    chunks = next(c for c in (4, 2, 1) if own % c == 0)
    per = own // chunks
    slot_count = assign.shape[1]
    hbm = pl.BlockSpec(memory_space=pltpu.HBM)
    vmem = pl.BlockSpec(memory_space=pltpu.VMEM)
    dma = pltpu.SemaphoreType.DMA
    across = max(b for b in range(1, n + 1) if n % b == 0 and b * b <= n)
    most = max(across, n // across)
    others = max(most - 1, 1)
    entry = (per * width, 2 * feat)
    return pl.pallas_call(
        functools.partial(kernel, n, across, groups, heads, chunks),
        out_shape=(
            pltpu.VMEM((1, slot_count * BLK, model), BF16),
            pltpu.VMEM((1, slot_count * BLK), F32),
        ),
        in_specs=[hbm] * 11,
        out_specs=(vmem, vmem),
        scratch_shapes=[
            pltpu.VMEM((n, chunks, BLK, model // chunks), BF16),
            pltpu.VMEM((rows, model), BF16),
            pltpu.VMEM((rows, model), BF16),
            pltpu.VMEM((rows, model), BF16),
            pltpu.VMEM((heads, width, feat), BF16),
            pltpu.VMEM((heads, width, feat), BF16),
            pltpu.VMEM((prows, model), BF16),
            pltpu.VMEM((prows, model), BF16),
            pltpu.VMEM((chunks, most, most, *entry), BF16),
            pltpu.VMEM((chunks, others, most, *entry), BF16),
            pltpu.VMEM((chunks, others, *entry), BF16),
            pltpu.VMEM((chunks, others, *entry), BF16),
            pltpu.VMEM((n, chunks, *entry), BF16),
            pltpu.VMEM((heads, 2 * feat), F32),
            pltpu.VMEM((across, heads, 2 * feat), BF16),
            pltpu.VMEM((n // across, heads, 2 * feat), BF16),
            pltpu.VMEM((heads, 2 * feat, rows), BF16),
            pltpu.VMEM((heads, width + EXTRA, rows), F32),
            pltpu.VMEM((chunks, n, BLK, model // chunks), BF16),
            pltpu.SMEM(prompt_len.shape, jnp.int32),
            pltpu.SMEM(resp_len.shape, jnp.int32),
            pltpu.SMEM(assign.shape, jnp.int32),
            pltpu.SMEM(rewards.shape, F32),
            pltpu.VMEM((n, 8, 128), jnp.int32),
            pltpu.VMEM((n, 8, 128), F32),
            pltpu.SMEM((n, 8, 128), jnp.int32),
            pltpu.VMEM((groups, 8, 128), F32),
            pltpu.VMEM((8, 128), F32),
            dma((chunks, 7)),
            dma((chunks,)),
            dma((chunks, most)),
            dma((chunks, most)),
            dma((chunks, most)),
            dma((chunks, most)),
            dma((n,)),
            dma((n,)),
            dma((chunks, n)),
            dma((chunks, n)),
            dma((chunks, n)),
            dma((chunks, n)),
            dma((2, n)),
            dma((2, n)),
            dma((groups,)),
            dma((groups,)),
            dma((n,)),
            dma,
            dma,
            dma((4,)),
            pltpu.SemaphoreType.REGULAR,
        ],
        compiler_params=pltpu.CompilerParams(
            collective_id=0, has_side_effects=True,
            vmem_limit_bytes=56 * 1024 * 1024,
        ),
        name="hedgehog",
    )(
        prompt_len, resp_len, assign, rewards, resp_q, resp_k, resp_v, prompt_k, prompt_v,
        feat_q, feat_k,
    )


def solution(mesh):
    return jax.shard_map(
        body,
        mesh=mesh,
        in_specs=(
            P("group", "dp", None),
            P("group", "dp", None),
            P("group", "dp", None),
            P("group", "dp", None),
            P("group", "dp", None),
            P("group"),
            P("group", "dp"),
            P("group", "dp"),
            P("group", "dp"),
            P(),
            P(),
        ),
        out_specs=(P("group", "dp", None), P("group", "dp")),
        check_vma=False,
    )
```
